256 devices in a mesh: cols: 8 (over x, z_hi), sites: 32 (over y, z_lo, core).
Axes of the slice: x: 4, y: 4, z: 8 (z_hi: 2, z_lo: 4; z = z_hi * 4 + z_lo), core: 2. Of those that a mesh axis runs over, the one named last changes fastest.
Arguments:
- right_vectors: float32 [2, 16, 8, 32, 256, 32], P(None, None, None, None, ('cols', 'sites')), may hold values from -6 to 6
- left_vectors: bfloat16 [2, 64, 512, 512], P(None, None, 'sites'), may hold values from -0.01171875 to 0.01171875
- vacancy: int32 [512, 512], P('sites'), may hold values 0 or 1
Outputs:
- gamma_moments: float32 [2, 4, 64, 16, 8], P(None, None, None, None, 'cols')
The draws below stay inside these ranges and needn't reach their ends.
All inputs are finite; a program needn't handle non-finite values. No bound on the sum of `vacancy` on one device may be relied on, other than what follows from the above.
Results may differ from the reference program's by a relative error of at most 0.0029.
Values sent between devices are 32-bit elements; how exact they have to be, the bound alone decides.
No kernel may reach another device: no remote copies, remote signals or barrier semaphores. Data moves between devices by JAX's collectives and lax.ppermute only.
A program may use at most 64 MiB of HBM per device.

```python
import jax
import jax.numpy as jnp
from jax import lax

COLS = 128
NL = 64
MOM = 4
LX = 512
RS = 16
LY = 512
CG = 16
PIECE = 32


def touch_ends(drawn, key, least, high):
    longest = drawn.shape.index(max(drawn.shape))
    spots = []
    for shift in (0, 1):
        where = [jax.random.randint(jax.random.fold_in(key, axis), (), 0, length) for axis, length in enumerate(drawn.shape)]
        where[longest] = (where[longest] + shift) % drawn.shape[longest]
        spots.append(tuple(where))
    return drawn.at[spots[0]].set(least).at[spots[1]].set(high)


def level_of(own_key, extent, pieces, least, top_value):
    loudness, own = 1.0, jax.random.fold_in(own_key, 6)
    for axis_at, blocks in pieces:
        steps = jnp.exp(jax.random.uniform(jax.random.fold_in(own, axis_at), (blocks,), jnp.float32, least / len(pieces), top_value / len(pieces)))
        loudness = loudness * jnp.repeat(steps, extent[axis_at] // blocks).reshape([-1 if axis == axis_at else 1 for axis in range(len(extent))])
    return loudness


def gaussian(key, extent, spread, limit, pieces=(), held_as=jnp.bfloat16):
    gain = level_of(key, extent, pieces, -0.22, 0.18) if pieces else 1.0
    entries = jax.random.normal(key, extent, jnp.float32) * spread * gain
    return jnp.minimum(jnp.maximum(entries, -limit), limit).astype(held_as)


def setup_inputs(seed: int = 0) -> dict:
    streams_of = jax.random.split(jax.random.key(seed), 4)
    return {
        "right_vectors": gaussian(streams_of[0], (2, CG, COLS // CG, LY // RS, (COLS // CG) * (LY // RS), PIECE), 1.0, 6.0, ((4, 256),), jnp.float32),
        "left_vectors": gaussian(streams_of[1], (2, NL, LY, LX), (LY * LX) ** -0.5, 0.01171875, ((2, 32),)),
        "vacancy": touch_ends((jax.random.randint(streams_of[2], (LY, LX), 0, 16) < 15).astype(jnp.int32), jax.random.fold_in(streams_of[2], 1), 0, 1),
    }


ONSITE_MASS = 0.3
SECOND_HOP = 0.2
BAND_SCALE = 4.5


def column_shift(values, offset):
    row_width = values.shape[-1]
    filler = jnp.zeros(values.shape[:-1] + (abs(offset),), values.dtype)
    if offset > 0:
        return jnp.concatenate([values[..., offset:], filler], axis=-1)
    return jnp.concatenate([filler, values[..., :row_width + offset]], axis=-1)


def rotate_phase(values):
    return jnp.stack([-values[1], values[0]])


def sign_table(row_count, row_width):
    rows_index = lax.broadcasted_iota(jnp.int32, (row_count, row_width), 0)
    cols_index = lax.broadcasted_iota(jnp.int32, (row_count, row_width), 1)
    return (1 - 2 * ((rows_index + cols_index) % 2)).astype(jnp.float32)


def haldane(padded, parity_sign):
    centre = padded[:, :, 1:-1, :]
    upper_row = padded[:, :, 2:, :]
    lower_row = padded[:, :, :-2, :]
    vertical = jnp.where(parity_sign > 0, upper_row, lower_row)
    nearest = column_shift(centre, 1) + column_shift(centre, -1) + vertical
    second = (column_shift(centre, 2) - column_shift(centre, -2) + column_shift(upper_row, -1)
              - column_shift(lower_row, 1) + column_shift(lower_row, -1) - column_shift(upper_row, 1))
    return ONSITE_MASS * parity_sign * centre + nearest + SECOND_HOP * parity_sign * rotate_phase(second)


def velocity(padded, parity_sign):
    centre = padded[:, :, 1:-1, :]
    upper_row = padded[:, :, 2:, :]
    lower_row = padded[:, :, :-2, :]
    along_x = column_shift(centre, 1) - column_shift(centre, -1)
    farther = column_shift(centre, 2) + column_shift(centre, -2)
    diagonal = (column_shift(upper_row, 1) + column_shift(upper_row, -1)
                + column_shift(lower_row, 1) + column_shift(lower_row, -1))
    return rotate_phase(along_x) - SECOND_HOP * parity_sign * (2.0 * farther - diagonal)


def wrap_rows(values):
    return jnp.concatenate([values[:, :, -1:, :], values, values[:, :, :1, :]], axis=2)


def reference(right_vectors, left_vectors, vacancy):
    group_count = COLS // CG
    columns = jnp.moveaxis(right_vectors.reshape(2, CG, group_count, LY, LX), 2, 0)
    present = vacancy.astype(jnp.float32)
    parity_sign = sign_table(LY, LX)
    left_matrix = left_vectors.astype(jnp.float32).reshape(2 * NL, LY * LX)

    def one_group(column_block):
        current = column_block * present
        latest = velocity(wrap_rows(current), parity_sign) * present
        previous = latest
        moment_list = [latest]
        for degree in range(1, MOM):
            applied = haldane(wrap_rows(latest), parity_sign) * present / BAND_SCALE
            following = applied if degree == 1 else 2.0 * applied - previous
            previous, latest = latest, following
            moment_list.append(latest)
        outputs = []
        for moment in moment_list:
            rounded = lax.optimization_barrier(moment.astype(jnp.bfloat16)).astype(jnp.float32)
            product = lax.dot_general(left_matrix, rounded.reshape(2 * CG, LY * LX),
                                      (((1,), (1,)), ((), ())),
                                      precision=lax.Precision.HIGHEST,
                                      preferred_element_type=jnp.float32).reshape(2, NL, 2, CG)
            outputs.append(jnp.stack([product[0, :, 0] + product[1, :, 1],
                                      product[0, :, 1] - product[1, :, 0]]))
        return jnp.stack(outputs, axis=1)

    gathered = lax.map(one_group, columns)
    return jnp.moveaxis(gathered, 0, -1)
```

```python
import jax
import jax.numpy as jnp
from jax import lax
from jax.experimental import pallas as pl
from jax.experimental.pallas import tpu as pltpu
from jax.sharding import PartitionSpec as P

MOM = 4
HALO = 4
ONSITE_MASS = 0.3
SECOND_HOP = 0.2
BAND_SCALE = 4.5
LANES = 128
SUB = 8
F32 = jnp.float32


def pack_kernel(in_ref, out_ref):
    slabs = out_ref.shape[0]
    for slab in range(slabs):
        parts = [in_ref[q * SUB : (q + 1) * SUB, slab, :] for q in range(4)]
        out_ref[slab] = jnp.concatenate(parts, axis=1)


def pack(pieces):
    rg, groups, slabs, width = pieces.shape
    return pl.pallas_call(
        pack_kernel,
        grid=(groups,),
        in_specs=[pl.BlockSpec((rg, None, slabs, width), lambda k: (0, k, 0, 0))],
        out_specs=pl.BlockSpec((slabs, SUB, LANES), lambda k: (k, 0, 0)),
        out_shape=jax.ShapeDtypeStruct((groups * slabs, SUB, LANES), F32),
        name="pack",
    )(pieces)


def shift_right_of(tiles, is_last):
    rolled = [pltpu.roll(t, LANES - 1, 1) for t in tiles]
    following = rolled[1:] + [jnp.zeros_like(rolled[0])]
    return [jnp.where(is_last, b, a) for a, b in zip(rolled, following)]


def shift_left_of(tiles, is_first):
    rolled = [pltpu.roll(t, 1, 1) for t in tiles]
    before = [jnp.zeros_like(rolled[0])] + rolled[:-1]
    return [jnp.where(is_first, b, a) for a, b in zip(rolled, before)]


def regroup(pieces, low_half, even_block):
    a = [None] * 4
    for p in (0, 1):
        a[p] = jnp.where(low_half, pieces[p], pltpu.roll(pieces[p + 2], 64, 1))
        a[p + 2] = jnp.where(low_half, pltpu.roll(pieces[p], 64, 1), pieces[p + 2])
    b = [None] * 4
    for p in (0, 2):
        b[p] = jnp.where(even_block, a[p], pltpu.roll(a[p + 1], 32, 1))
        b[p + 1] = jnp.where(even_block, pltpu.roll(a[p], 96, 1), a[p + 1])
    return b


def moments_kernel(recv_ref, lo_ref, hi_ref, pres_ref, left_ref, out_ref, field, mrow):
    rows = left_ref.shape[0]
    ext = rows + 2 * HALO
    width = left_ref.shape[2]
    tiles = width // LANES
    lane = lax.broadcasted_iota(jnp.int32, (SUB, LANES), 1)
    low_half = lane < 64
    even_block = (lane // 32) % 2 == 0
    is_first = lane == 0
    is_last = lane == LANES - 1
    even_lane = lane % 2 == 0
    plus = jnp.where(even_lane, 1.0, -1.0).astype(F32)

    def load(ref, lead):
        return [ref[(*lead, slice(None), pl.ds(t * LANES, LANES))] for t in range(tiles)]

    def store(ref, lead, values):
        for t in range(tiles):
            ref[(*lead, slice(None), pl.ds(t * LANES, LANES))] = values[t]

    def unpack_row(src, src_row, e):
        pres = load(pres_ref, (e,))
        for t in range(tiles):
            pieces = [src[src_row * 16 + t * 4 + p] for p in range(4)]
            for q, value in enumerate(regroup(pieces, low_half, even_block)):
                field[0, e, q // 2, q % 2, :, pl.ds(t * LANES, LANES)] = value * pres[t]

    @pl.loop(0, HALO)
    def _(i):
        unpack_row(lo_ref, i, i)
        unpack_row(hi_ref, i, rows + HALO + i)

    @pl.loop(0, rows)
    def _(i):
        unpack_row(recv_ref, i, i + HALO)

    def row(level, e, parity, half):
        sign = plus if parity == 0 else -plus
        up_mask = even_lane if parity == 0 else jnp.logical_not(even_lane)
        c = [load(field, (level, e, r, half)) for r in (0, 1)]
        u = [load(field, (level, e + 1, r, half)) for r in (0, 1)]
        l = [load(field, (level, e - 1, r, half)) for r in (0, 1)]
        pres = load(pres_ref, (e,))
        f = [[sign * a for a in c[r]] for r in (0, 1)]
        d = [[sign * (a + b) for a, b in zip(u[r], l[r])] for r in (0, 1)]
        fr = [shift_right_of(f[r], is_last) for r in (0, 1)]
        fl = [shift_left_of(f[r], is_first) for r in (0, 1)]
        T = range(tiles)
        if level == 0:
            right = [
                [-c[1][t] - SECOND_HOP * d[0][t] - 2 * SECOND_HOP * fr[0][t] for t in T],
                [c[0][t] - SECOND_HOP * d[1][t] - 2 * SECOND_HOP * fr[1][t] for t in T],
            ]
            left = [
                [c[1][t] - SECOND_HOP * d[0][t] - 2 * SECOND_HOP * fl[0][t] for t in T],
                [-c[0][t] - SECOND_HOP * d[1][t] - 2 * SECOND_HOP * fl[1][t] for t in T],
            ]
        else:
            right = [
                [c[0][t] - SECOND_HOP * (d[1][t] + fr[1][t]) for t in T],
                [c[1][t] + SECOND_HOP * (d[0][t] + fr[0][t]) for t in T],
            ]
            left = [
                [c[0][t] + SECOND_HOP * (d[1][t] + fl[1][t]) for t in T],
                [c[1][t] - SECOND_HOP * (d[0][t] + fl[0][t]) for t in T],
            ]
        result = []
        for r in (0, 1):
            a = shift_right_of(right[r], is_last)
            b = shift_left_of(left[r], is_first)
            total = [a[t] + b[t] for t in T]
            if level > 0:
                vert = [jnp.where(up_mask, u[r][t], l[r][t]) for t in T]
                total = [total[t] + (ONSITE_MASS * f[r][t] + vert[t]) for t in T]
                scale = 1.0 / BAND_SCALE if level == 1 else 2.0 / BAND_SCALE
                total = [total[t] * (scale * pres[t]) for t in T]
                if level > 1:
                    old = load(field, (level - 1, e, r, half))
                    total = [total[t] - old[t] for t in T]
            else:
                total = [total[t] * pres[t] for t in T]
            result.append(total)
        return result

    for level in range(MOM):
        reach = HALO - 1 - level
        first = HALO - reach
        @pl.loop(0, (rows + 2 * reach) // 2)
        def _(i, level=level, first=first):
            for k in (0, 1):
                e = first + 2 * i + k
                for half in (0, 1):
                    values = row(level, e, (first + k) % 2, half)
                    if level < MOM - 1:
                        for r in (0, 1):
                            store(field, (level + 1, e, r, half), values[r])
                    else:
                        for r in (0, 1):
                            store(mrow, (e - HALO, r, half), values[r])

    acc = jnp.zeros((2 * left_ref.shape[1] // 2, left_ref.shape[1]), F32)

    def product(y, acc):
        stacked = []
        for r in (0, 1):
            for m in range(MOM):
                for half in (0, 1):
                    if m < MOM - 1:
                        stacked.append(field[m + 1, y + HALO, r, half])
                    else:
                        stacked.append(mrow[y, r, half])
        rhs = jnp.concatenate(stacked, axis=0).astype(jnp.bfloat16)
        return acc + lax.dot_general(
            rhs, left_ref[y], (((1,), (1,)), ((), ())), preferred_element_type=F32
        )

    acc = lax.fori_loop(0, rows, product, jnp.zeros((2 * MOM * 2 * SUB, left_ref.shape[1]), F32))
    half_rows = MOM * 2 * SUB
    top, bottom = acc[:half_rows], acc[half_rows:]
    lane_out = lax.broadcasted_iota(jnp.int32, top.shape, 1)
    out_ref[...] = pltpu.roll(bottom, 64, 1) + jnp.where(lane_out < 64, top, -top)


def moments(recv, lo, hi, pres, left):
    rows, n2, width = left.shape
    ext = rows + 2 * HALO
    vm = pl.BlockSpec(memory_space=pltpu.VMEM)
    return pl.pallas_call(
        moments_kernel,
        in_specs=[vm] * 5,
        out_specs=vm,
        out_shape=jax.ShapeDtypeStruct((MOM * 2 * SUB, n2), F32),
        scratch_shapes=[
            pltpu.VMEM((MOM, ext, 2, 2, SUB, width), F32),
            pltpu.VMEM((rows, 2, 2, SUB, width), F32),
        ],
        compiler_params=pltpu.CompilerParams(vmem_limit_bytes=40 * 2**20),
        name="moments",
    )(recv, lo, hi, pres, left)


def per_device(right_vectors, left_vectors, vacancy):
    parts, width_group, groups, slabs, _, piece = right_vectors.shape
    count = lax.axis_size("sites")
    up = [(i, (i + 1) % count) for i in range(count)]
    down = [((i + 1) % count, i) for i in range(count)]
    n_left, rows, width = left_vectors.shape[1:]

    present = vacancy.astype(F32)
    pres_ext = jnp.concatenate(
        [
            lax.ppermute(present[rows - HALO :], "sites", up),
            present,
            lax.ppermute(present[:HALO], "sites", down),
        ],
        axis=0,
    )
    pres_ext = jnp.broadcast_to(pres_ext[:, None, :], (rows + 2 * HALO, SUB, width))
    left = jnp.swapaxes(left_vectors.reshape(2 * n_left, rows, width), 0, 1)

    packed = pack(right_vectors.reshape(parts * width_group, groups, slabs, piece))
    recv = lax.all_to_all(packed, ("cols", "sites"), 0, 0, tiled=True)
    edge = HALO * width // piece
    lo = lax.ppermute(recv[recv.shape[0] - edge :], "sites", up)
    hi = lax.ppermute(recv[:edge], "sites", down)
    total = moments(recv, lo, hi, pres_ext, left)
    step = 1
    while step < count:
        total = total + lax.ppermute(total, "sites", [(i, i ^ step) for i in range(count)])
        step *= 2
    out = total.reshape(MOM, width_group, 2, n_left)
    return jnp.transpose(out, (2, 0, 3, 1))[..., None]


def solution(mesh):
    return jax.shard_map(
        per_device,
        mesh=mesh,
        in_specs=(
            P(None, None, None, None, ("cols", "sites"), None),
            P(None, None, "sites", None),
            P("sites", None),
        ),
        out_specs=P(None, None, None, None, "cols"),
        check_vma=False,
    )
```

```python
import jax
import jax.numpy as jnp
from jax import lax
from jax.experimental import pallas as pl
from jax.experimental.pallas import tpu as pltpu
from jax.sharding import PartitionSpec as P

MOM = 4
HALO = 4
ONSITE_MASS = 0.3
SECOND_HOP = 0.2
BAND_SCALE = 4.5
LANES = 128
SUB = 8
TILES = 4
F32 = jnp.float32


def pack_kernel(in_ref, out_ref):
    lane = lax.broadcasted_iota(jnp.int32, (SUB, LANES), 1)
    source = lane // 32 * 32 + lane % 8 * 4 + lane // 8 % 4
    slabs = out_ref.shape[0]
    for slab in range(slabs):
        parts = [in_ref[q * SUB : (q + 1) * SUB, slab, :] for q in range(4)]
        tile = jnp.concatenate(parts, axis=1)
        out_ref[slab] = jnp.take_along_axis(tile, source, axis=1)


def pack(pieces):
    rg, groups, slabs, width = pieces.shape
    return pl.pallas_call(
        pack_kernel,
        grid=(groups,),
        in_specs=[pl.BlockSpec((rg, None, slabs, width), lambda k: (0, k, 0, 0))],
        out_specs=pl.BlockSpec((slabs, SUB, LANES), lambda k: (k, 0, 0)),
        out_shape=jax.ShapeDtypeStruct((groups * slabs, SUB, LANES), F32),
        name="pack",
    )(pieces)


def regroup(pieces, block_bits):
    tiles = list(pieces)
    for bit, is_set in enumerate(block_bits):
        step = 1 << bit
        for p in range(16):
            if p & step:
                continue
            low, high = tiles[p], tiles[p | step]
            tiles[p] = jnp.where(is_set, pltpu.roll(high, SUB * step, 1), low)
            tiles[p | step] = jnp.where(is_set, high, pltpu.roll(low, LANES - SUB * step, 1))
    return tiles


def moments_kernel(recv_ref, lo_ref, hi_ref, pres_ref, left_ref, out_ref, field, presb):
    rows = left_ref.shape[0]
    lane = lax.broadcasted_iota(jnp.int32, (SUB, LANES), 1)
    block_bits = [(lane // SUB >> bit) % 2 == 1 for bit in range(4)]
    is_first = lane == 0
    is_last = lane == LANES - 1
    T = range(TILES)
    edge = HALO * 16

    def unpack_row(src, src_row, e, mask_rows):
        for t in T:
            presb[e, t] = jnp.broadcast_to(mask_rows[t], (SUB, LANES))
        pieces = [src[src_row * 16 + b] for b in range(16)]
        for v, value in enumerate(regroup(pieces, block_bits)):
            field[0, e, v // 8, v // 4 % 2, v % 4] = value * presb[e, v % 4]

    for i in range(HALO):
        for src, e in ((lo_ref, i), (hi_ref, rows + HALO + i)):
            at = [i * TILES + t for t in T]
            unpack_row(src, i, e, [src[edge + a // SUB, pl.ds(a % SUB, 1), :] for a in at])

    @pl.loop(0, rows)
    def _(i):
        unpack_row(recv_ref, i, i + HALO, [pres_ref[i, pl.ds(t, 1), :] for t in T])

    def ahead(tiles):
        wrapped = jnp.where(is_last, 0.0, pltpu.roll(tiles[0], LANES - 1, 1))
        return tiles[1:] + [wrapped]

    def behind(tiles):
        wrapped = jnp.where(is_first, 0.0, pltpu.roll(tiles[-1], 1, 1))
        return [wrapped] + tiles[:-1]

    def row(level, parity, below, centre, above, mask):
        c, d, nxt, prv, second = [], [], [], [], []
        for r in (0, 1):
            w = centre[r]
            diag = [above[r][t] + below[r][t] for t in T]
            fore, back = ahead(w), behind(w)
            if level == 0:
                a = ahead([2.0 * fore[t] - diag[t] for t in T])
                b = behind([2.0 * back[t] - diag[t] for t in T])
                second.append([a[t] + b[t] for t in T])
            else:
                a = ahead([fore[t] - diag[t] for t in T])
                b = behind([back[t] - diag[t] for t in T])
                second.append([a[t] - b[t] for t in T])
            nxt.append(fore)
            prv.append(back)
        result = []
        for r in (0, 1):
            values = []
            for t in T:
                sign = 1.0 if (parity + t) % 2 == 0 else -1.0
                if level == 0:
                    if r == 0:
                        along = prv[1][t] - nxt[1][t]
                    else:
                        along = nxt[0][t] - prv[0][t]
                    total = along - (SECOND_HOP * sign) * second[r][t]
                else:
                    vertical = above[r][t] if sign > 0 else below[r][t]
                    near = (nxt[r][t] + prv[r][t]) + vertical
                    turn = -sign if r == 0 else sign
                    total = near + (
                        (ONSITE_MASS * sign) * centre[r][t] + (SECOND_HOP * turn) * second[1 - r][t]
                    )
                values.append(total * mask[t])
            result.append(values)
        return result

    def load(level, e, half):
        return [[field[level, e, r, half, t] for t in T] for r in (0, 1)]

    for level in range(MOM):
        reach = HALO - 1 - level
        first = HALO - reach

        @pl.loop(0, (rows + 2 * reach) // 2)
        def _(i, level=level, first=first):
            e = first + 2 * i
            scale = (1.0, 1.0 / BAND_SCALE, 2.0 / BAND_SCALE, 2.0 / BAND_SCALE)[level]
            masks = []
            for k in (0, 1):
                mask = [presb[e + k, t] for t in T]
                masks.append(mask if level == 0 else [scale * m for m in mask])
            for half in (0, 1):
                window = [load(level, e + k, half) for k in (-1, 0, 1, 2)]
                for k in (0, 1):
                    values = row(level, (first + k) % 2, *window[k : k + 3], masks[k])
                    if level > 1:
                        old = load(level - 1, e + k, half)
                        values = [[values[r][t] - old[r][t] for t in T] for r in (0, 1)]
                    for r in (0, 1):
                        for t in T:
                            field[(level + 1) % MOM, e + k, r, half, t] = values[r][t]

    acc = None
    for y in range(rows):
        for t in T:
            rhs = jnp.concatenate(
                [field[(m + 1) % MOM, y + HALO, r, half, t] for r in (0, 1) for m in range(MOM) for half in (0, 1)],
                axis=0,
            ).astype(jnp.bfloat16)
            term = lax.dot_general(
                rhs,
                left_ref[y, :, t * LANES : (t + 1) * LANES],
                (((1,), (1,)), ((), ())),
                preferred_element_type=F32,
            )
            acc = term if acc is None else acc + term
    half_rows = MOM * 2 * SUB
    top, bottom = acc[:half_rows], acc[half_rows:]
    lane_out = lax.broadcasted_iota(jnp.int32, top.shape, 1)
    out_ref[...] = pltpu.roll(bottom, 64, 1) + jnp.where(lane_out < 64, top, -top)


def moments(recv, lo, hi, pres, left):
    rows, n2, width = left.shape
    ext = rows + 2 * HALO
    vm = pl.BlockSpec(memory_space=pltpu.VMEM)
    return pl.pallas_call(
        moments_kernel,
        in_specs=[vm] * 5,
        out_specs=vm,
        out_shape=jax.ShapeDtypeStruct((MOM * 2 * SUB, n2), F32),
        scratch_shapes=[
            pltpu.VMEM((MOM, ext, 2, 2, TILES, SUB, LANES), F32),
            pltpu.VMEM((ext, TILES, SUB, LANES), F32),
        ],
        compiler_params=pltpu.CompilerParams(vmem_limit_bytes=40 * 2**20),
        name="moments",
    )(recv, lo, hi, pres, left)


def per_device(right_vectors, left_vectors, vacancy):
    parts, width_group, groups, slabs, _, piece = right_vectors.shape
    count = lax.axis_size("sites")
    up = [(i, (i + 1) % count) for i in range(count)]
    down = [((i + 1) % count, i) for i in range(count)]
    n_left, rows, width = left_vectors.shape[1:]

    packed = pack(right_vectors.reshape(parts * width_group, groups, slabs, piece))
    packed, left_vectors = lax.optimization_barrier((packed, left_vectors))
    recv = lax.all_to_all(packed, ("cols", "sites"), 0, 0, tiled=True)

    site = lax.broadcasted_iota(jnp.int32, (width, width), 0)
    place = lax.broadcasted_iota(jnp.int32, (width, width), 1)
    to_place = (site % TILES * LANES + site // TILES == place).astype(jnp.bfloat16)
    left = left_vectors.reshape(2 * n_left * rows, width)
    left = jnp.dot(left, to_place, preferred_element_type=jnp.bfloat16)
    left = jnp.swapaxes(left.reshape(2 * n_left, rows, width), 0, 1)
    present = jnp.dot(vacancy.astype(jnp.bfloat16), to_place, preferred_element_type=F32)
    present = present.reshape(rows, TILES, LANES)
    recv, left, present = lax.optimization_barrier((recv, left, present))

    edge = HALO * width // piece
    low_mask = present[:HALO].reshape(-1, SUB, LANES)
    high_mask = present[rows - HALO :].reshape(-1, SUB, LANES)
    lo = lax.ppermute(jnp.concatenate([recv[recv.shape[0] - edge :], high_mask]), "sites", up)
    hi = lax.ppermute(jnp.concatenate([recv[:edge], low_mask]), "sites", down)
    total = moments(recv, lo, hi, present, left)
    step = 1
    while step < count:
        total = total + lax.ppermute(total, "sites", [(i, i ^ step) for i in range(count)])
        step *= 2
    out = total.reshape(MOM, width_group, 2, n_left)
    return jnp.transpose(out, (2, 0, 3, 1))[..., None]


def solution(mesh):
    return jax.shard_map(
        per_device,
        mesh=mesh,
        in_specs=(
            P(None, None, None, None, ("cols", "sites"), None),
            P(None, None, "sites", None),
            P("sites", None),
        ),
        out_specs=P(None, None, None, None, "cols"),
        check_vma=False,
    )
```

```python
import jax
import jax.numpy as jnp
from jax import lax
from jax.experimental import pallas as pl
from jax.experimental.pallas import tpu as pltpu
from jax.sharding import PartitionSpec as P

MOM = 4
HALO = 4
ONSITE_MASS = 0.3
SECOND_HOP = 0.2
BAND_SCALE = 4.5
LANES = 128
SUB = 8
GROUPSTEP = 2
TILES = 4
F32 = jnp.float32


def pack_kernel(in_ref, out_ref, turned):
    columns, groups, slabs, width = in_ref.shape
    block = lax.broadcasted_iota(jnp.int32, (SUB, LANES), 1) // width
    odd, high = block % 2 == 1, block >= 2
    lane = lax.broadcasted_iota(jnp.int32, (SUB, LANES), 1)
    swapped = jnp.where(odd, lane - width, lane + width)
    spots = [(k, base) for k in range(groups) for base in range(0, slabs, 4)]
    for slot, (k, base) in enumerate(spots):
        if base % 8 == 0:
            octets = [jnp.swapaxes(in_ref[c : c + SUB, k, base : base + SUB, :], 0, 1) for c in range(0, columns, SUB)]
        rows = [octets[c][base % 8 + s] for s in range(4) for c in range(columns // SUB)]
        turned[slot] = jnp.concatenate(rows, axis=0).T
    for slot, (k, base) in enumerate(spots):
        v = [turned[slot, pl.ds(t, SUB, stride=TILES), :] for t in range(TILES)]
        for p in (0, 2):
            low, upper = v[p], v[p + 1]
            moved = jnp.take_along_axis(jnp.where(odd, low, upper), swapped, axis=1)
            v[p], v[p + 1] = jnp.where(odd, moved, low), jnp.where(odd, upper, moved)
        for p in (0, 1):
            low, upper = v[p], v[p + 2]
            moved = pltpu.roll(jnp.where(high, low, upper), LANES // 2, 1)
            v[p], v[p + 2] = jnp.where(high, moved, low), jnp.where(high, upper, moved)
        for s in range(4):
            out_ref[k, base + s] = v[s]


def pack(pieces):
    columns, groups, slabs, width = pieces.shape
    step = GROUPSTEP
    out = pl.pallas_call(
        pack_kernel,
        grid=(groups // step,),
        in_specs=[pl.BlockSpec((columns, step, slabs, width), lambda k: (0, k, 0, 0))],
        out_specs=pl.BlockSpec((step, slabs, SUB, LANES), lambda k: (k, 0, 0, 0)),
        out_shape=jax.ShapeDtypeStruct((groups, slabs, SUB, LANES), F32),
        scratch_shapes=[pltpu.VMEM((step * slabs // 4, width, LANES), F32)],
        compiler_params=pltpu.CompilerParams(vmem_limit_bytes=40 * 2**20),
        name="pack",
    )(pieces)
    return out.reshape(groups * slabs, SUB, LANES)


def moments_kernel(recv_ref, lo_ref, hi_ref, pres_ref, left_ref, out_ref, field, presb):
    rows = left_ref.shape[0]
    lane = lax.broadcasted_iota(jnp.int32, (SUB, LANES), 1)
    is_first = lane == 0
    is_last = lane == LANES - 1
    T = range(TILES)
    edge = HALO * 16

    def unpack_row(src, src_row, e, mask_rows):
        for t in T:
            presb[e, t] = jnp.broadcast_to(mask_rows[t], (SUB, LANES))
        turned = src[pl.ds(src_row * 16, 16)].reshape(LANES, LANES).T
        for t in T:
            for q in range(4):
                at = (4 * t + q) * SUB
                field[0, e, q // 2, q % 2, t] = turned[at : at + SUB] * presb[e, t]

    for i in range(HALO):
        for src, e in ((lo_ref, i), (hi_ref, rows + HALO + i)):
            at = [i * TILES + t for t in T]
            unpack_row(src, i, e, [src[edge + a // SUB, pl.ds(a % SUB, 1), :] for a in at])

    @pl.loop(0, rows // 4)
    def _(i):
        for k in range(4):
            y = 4 * i + k
            unpack_row(recv_ref, y, y + HALO, [pres_ref[y, pl.ds(t, 1), :] for t in T])

    def ahead(tiles):
        wrapped = jnp.where(is_last, 0.0, pltpu.roll(tiles[0], LANES - 1, 1))
        return tiles[1:] + [wrapped]

    def behind(tiles):
        wrapped = jnp.where(is_first, 0.0, pltpu.roll(tiles[-1], 1, 1))
        return [wrapped] + tiles[:-1]

    def row(level, parity, below, centre, above, mask):
        c, d, nxt, prv, second = [], [], [], [], []
        for r in (0, 1):
            w = centre[r]
            diag = [above[r][t] + below[r][t] for t in T]
            fore, back = ahead(w), behind(w)
            if level == 0:
                a = ahead([2.0 * fore[t] - diag[t] for t in T])
                b = behind([2.0 * back[t] - diag[t] for t in T])
                second.append([a[t] + b[t] for t in T])
            else:
                a = ahead([fore[t] - diag[t] for t in T])
                b = behind([back[t] - diag[t] for t in T])
                second.append([a[t] - b[t] for t in T])
            nxt.append(fore)
            prv.append(back)
        result = []
        for r in (0, 1):
            values = []
            for t in T:
                sign = 1.0 if (parity + t) % 2 == 0 else -1.0
                if level == 0:
                    if r == 0:
                        along = prv[1][t] - nxt[1][t]
                    else:
                        along = nxt[0][t] - prv[0][t]
                    total = along - (SECOND_HOP * sign) * second[r][t]
                else:
                    vertical = above[r][t] if sign > 0 else below[r][t]
                    near = (nxt[r][t] + prv[r][t]) + vertical
                    turn = -sign if r == 0 else sign
                    total = near + (
                        (ONSITE_MASS * sign) * centre[r][t] + (SECOND_HOP * turn) * second[1 - r][t]
                    )
                values.append(total * mask[t])
            result.append(values)
        return result

    def load(level, e, half):
        return [[field[level, e, r, half, t] for t in T] for r in (0, 1)]

    for level in range(MOM):
        reach = HALO - 1 - level
        first = HALO - reach

        @pl.loop(0, (rows + 2 * reach) // 2)
        def _(i, level=level, first=first):
            e = first + 2 * i
            scale = (1.0, 1.0 / BAND_SCALE, 2.0 / BAND_SCALE, 2.0 / BAND_SCALE)[level]
            masks = []
            for k in (0, 1):
                mask = [presb[e + k, t] for t in T]
                masks.append(mask if level == 0 else [scale * m for m in mask])
            for half in (0, 1):
                window = [load(level, e + k, half) for k in (-1, 0, 1, 2)]
                for k in (0, 1):
                    values = row(level, (first + k) % 2, *window[k : k + 3], masks[k])
                    if level > 1:
                        old = load(level - 1, e + k, half)
                        values = [[values[r][t] - old[r][t] for t in T] for r in (0, 1)]
                    for r in (0, 1):
                        for t in T:
                            field[(level + 1) % MOM, e + k, r, half, t] = values[r][t]

    acc = None
    for y in range(rows):
        for t in T:
            rhs = jnp.concatenate(
                [field[(m + 1) % MOM, y + HALO, r, half, t] for r in (0, 1) for m in range(MOM) for half in (0, 1)],
                axis=0,
            ).astype(jnp.bfloat16)
            term = lax.dot_general(
                rhs,
                left_ref[y, :, t * LANES : (t + 1) * LANES],
                (((1,), (1,)), ((), ())),
                preferred_element_type=F32,
            )
            acc = term if acc is None else acc + term
    half_rows = MOM * 2 * SUB
    top, bottom = acc[:half_rows], acc[half_rows:]
    lane_out = lax.broadcasted_iota(jnp.int32, top.shape, 1)
    out_ref[...] = pltpu.roll(bottom, 64, 1) + jnp.where(lane_out < 64, top, -top)


def moments(recv, lo, hi, pres, left):
    rows, n2, width = left.shape
    ext = rows + 2 * HALO
    vm = pl.BlockSpec(memory_space=pltpu.VMEM)
    return pl.pallas_call(
        moments_kernel,
        in_specs=[vm] * 5,
        out_specs=vm,
        out_shape=jax.ShapeDtypeStruct((MOM * 2 * SUB, n2), F32),
        scratch_shapes=[
            pltpu.VMEM((MOM, ext, 2, 2, TILES, SUB, LANES), F32),
            pltpu.VMEM((ext, TILES, SUB, LANES), F32),
        ],
        compiler_params=pltpu.CompilerParams(vmem_limit_bytes=40 * 2**20),
        name="moments",
    )(recv, lo, hi, pres, left)


def per_device(right_vectors, left_vectors, vacancy):
    parts, width_group, groups, slabs, _, piece = right_vectors.shape
    count = lax.axis_size("sites")
    up = [(i, (i + 1) % count) for i in range(count)]
    down = [((i + 1) % count, i) for i in range(count)]
    n_left, rows, width = left_vectors.shape[1:]

    packed = pack(right_vectors.reshape(parts * width_group, groups, slabs, piece))
    packed, left_vectors = lax.optimization_barrier((packed, left_vectors))
    recv = lax.all_to_all(packed, ("cols", "sites"), 0, 0, tiled=True)

    site = lax.broadcasted_iota(jnp.int32, (width, width), 0)
    place = lax.broadcasted_iota(jnp.int32, (width, width), 1)
    to_place = (site % TILES * LANES + site // TILES == place).astype(jnp.bfloat16)
    left = left_vectors.reshape(2 * n_left * rows, width)
    left = jnp.dot(left, to_place, preferred_element_type=jnp.bfloat16)
    left = jnp.swapaxes(left.reshape(2 * n_left, rows, width), 0, 1)
    present = jnp.dot(vacancy.astype(jnp.bfloat16), to_place, preferred_element_type=F32)
    present = present.reshape(rows, TILES, LANES)
    recv, left, present = lax.optimization_barrier((recv, left, present))

    edge = HALO * width // piece
    low_mask = present[:HALO].reshape(-1, SUB, LANES)
    high_mask = present[rows - HALO :].reshape(-1, SUB, LANES)
    lo = lax.ppermute(jnp.concatenate([recv[recv.shape[0] - edge :], high_mask]), "sites", up)
    hi = lax.ppermute(jnp.concatenate([recv[:edge], low_mask]), "sites", down)
    total = moments(recv, lo, hi, present, left)
    step = 1
    while step < count:
        total = total + lax.ppermute(total, "sites", [(i, i ^ step) for i in range(count)])
        step *= 2
    out = total.reshape(MOM, width_group, 2, n_left)
    return jnp.transpose(out, (2, 0, 3, 1))[..., None]


def solution(mesh):
    return jax.shard_map(
        per_device,
        mesh=mesh,
        in_specs=(
            P(None, None, None, None, ("cols", "sites"), None),
            P(None, None, "sites", None),
            P("sites", None),
        ),
        out_specs=P(None, None, None, None, "cols"),
        check_vma=False,
    )
```

```python
import jax
import jax.numpy as jnp
from jax import lax
from jax.experimental import pallas as pl
from jax.experimental.pallas import tpu as pltpu
from jax.sharding import PartitionSpec as P

MOM = 4
HALO = 4
ONSITE_MASS = 0.3
SECOND_HOP = 0.2
BAND_SCALE = 4.5
LANES = 128
SUB = 8
TILES = 4
F32 = jnp.float32


def pack_kernel(in_ref, out_ref, turned):
    columns, groups, slabs, width = in_ref.shape
    block = lax.broadcasted_iota(jnp.int32, (SUB, LANES), 1) // width
    odd, high = block % 2 == 1, block >= 2
    lane = lax.broadcasted_iota(jnp.int32, (SUB, LANES), 1)
    swapped = jnp.where(odd, lane - width, lane + width)
    spots = [(k, base) for k in range(groups) for base in range(0, slabs, 4)]
    for slot, (k, base) in enumerate(spots):
        if base % 8 == 0:
            octets = [jnp.swapaxes(in_ref[c : c + SUB, k, base : base + SUB, :], 0, 1) for c in range(0, columns, SUB)]
        rows = [octets[c][base % 8 + s] for s in range(4) for c in range(columns // SUB)]
        turned[slot] = jnp.concatenate(rows, axis=0).T
    for slot, (k, base) in enumerate(spots):
        v = [turned[slot, pl.ds(t, SUB, stride=TILES), :] for t in range(TILES)]
        for p in (0, 2):
            low, upper = v[p], v[p + 1]
            moved = jnp.take_along_axis(jnp.where(odd, low, upper), swapped, axis=1)
            v[p], v[p + 1] = jnp.where(odd, moved, low), jnp.where(odd, upper, moved)
        for p in (0, 1):
            low, upper = v[p], v[p + 2]
            moved = pltpu.roll(jnp.where(high, low, upper), LANES // 2, 1)
            v[p], v[p + 2] = jnp.where(high, moved, low), jnp.where(high, upper, moved)
        for s in range(4):
            out_ref[k, base + s] = v[s]


def pack(pieces):
    columns, groups, slabs, width = pieces.shape
    step = 2
    out = pl.pallas_call(
        pack_kernel,
        grid=(groups // step,),
        in_specs=[pl.BlockSpec((columns, step, slabs, width), lambda k: (0, k, 0, 0))],
        out_specs=pl.BlockSpec((step, slabs, SUB, LANES), lambda k: (k, 0, 0, 0)),
        out_shape=jax.ShapeDtypeStruct((groups, slabs, SUB, LANES), F32),
        scratch_shapes=[pltpu.VMEM((step * slabs // 4, width, LANES), F32)],
        name="pack",
    )(pieces)
    return out.reshape(groups * slabs, SUB, LANES)


def wrap_masks():
    lane = lax.broadcasted_iota(jnp.int32, (SUB, LANES), 1)
    return lane == 0, lane == LANES - 1


def ahead(tiles, is_last):
    wrapped = jnp.where(is_last, 0.0, pltpu.roll(tiles[0], LANES - 1, 1))
    return tiles[1:] + [wrapped]


def behind(tiles, is_first):
    wrapped = jnp.where(is_first, 0.0, pltpu.roll(tiles[-1], 1, 1))
    return [wrapped] + tiles[:-1]


def stencil_row(level, parity, below, centre, above, old, mask, wraps):
    is_first, is_last = wraps
    T = range(TILES)
    nxt, prv, second = [], [], []
    for r in (0, 1):
        w = centre[r]
        diag = [above[r][t] + below[r][t] for t in T]
        fore, back = ahead(w, is_last), behind(w, is_first)
        if level == 0:
            a = ahead([2.0 * fore[t] - diag[t] for t in T], is_last)
            b = behind([2.0 * back[t] - diag[t] for t in T], is_first)
            second.append([a[t] + b[t] for t in T])
        else:
            a = ahead([fore[t] - diag[t] for t in T], is_last)
            b = behind([back[t] - diag[t] for t in T], is_first)
            second.append([a[t] - b[t] for t in T])
        nxt.append(fore)
        prv.append(back)
    result = []
    for r in (0, 1):
        values = []
        for t in T:
            sign = 1.0 if (parity + t) % 2 == 0 else -1.0
            if level == 0:
                along = prv[1][t] - nxt[1][t] if r == 0 else nxt[0][t] - prv[0][t]
                total = along - (SECOND_HOP * sign) * second[r][t]
            else:
                vertical = above[r][t] if sign > 0 else below[r][t]
                near = (nxt[r][t] + prv[r][t]) + vertical
                turn = -sign if r == 0 else sign
                total = near + (
                    (ONSITE_MASS * sign) * centre[r][t] + (SECOND_HOP * turn) * second[1 - r][t]
                )
            total = total * mask[t]
            values.append(total - old[r][t] if level > 1 else total)
        result.append(values)
    return result


SCALES = (1.0, 1.0 / BAND_SCALE, 2.0 / BAND_SCALE, 2.0 / BAND_SCALE)


def scaled(level, mask):
    return mask if level == 0 else [SCALES[level] * m for m in mask]


def turn_row(src, first):
    return src[pl.ds(first, 16)].reshape(LANES, LANES).T


def product(acc, blocks, left_ref, y):
    for t in range(TILES):
        zero = jnp.zeros((SUB, LANES), F32)
        stacked = [blocks(r, m, h, t) for r in (0, 1) for m in range(MOM) for h in (0, 1)]
        rhs = jnp.concatenate([zero if b is None else b for b in stacked], axis=0)
        term = lax.dot_general(
            rhs.astype(jnp.bfloat16),
            left_ref[y, :, t * LANES : (t + 1) * LANES],
            (((1,), (1,)), ((), ())),
            preferred_element_type=F32,
        )
        acc = term if acc is None else acc + term
    return acc


def inner_kernel(recv_ref, pres_ref, left_ref, sum_ref, edge_ref, field, presb):
    rows = left_ref.shape[0]
    wraps = wrap_masks()
    T = range(TILES)

    @pl.loop(0, rows // 4)
    def _(i):
        for k in range(4):
            y = 4 * i + k
            turned = turn_row(recv_ref, y * 16)
            for t in T:
                mask = jnp.broadcast_to(pres_ref[y, pl.ds(t, 1), :], (SUB, LANES))
                presb[y, t] = mask
                for q in range(4):
                    at = (4 * t + q) * SUB
                    field[0, y, q // 2, q % 2, t] = turned[at : at + SUB] * mask

    def load(level, y, half):
        return [[field[level, y, r, half, t] for t in T] for r in (0, 1)]

    for level in range(MOM):
        first = level + 1

        @pl.loop(0, (rows - 2 * first) // 2)
        def _(i, level=level, first=first):
            y = first + 2 * i
            masks = [scaled(level, [presb[y + k, t] for t in T]) for k in (0, 1)]
            for half in (0, 1):
                window = [load(level, y + k, half) for k in (-1, 0, 1, 2)]
                for k in (0, 1):
                    old = load(level - 1, y + k, half) if level > 1 else None
                    values = stencil_row(
                        level, (first + k) % 2, *window[k : k + 3], old, masks[k], wraps
                    )
                    for r in (0, 1):
                        for t in T:
                            field[(level + 1) % MOM, y + k, r, half, t] = values[r][t]

    for level in range(MOM):
        edge_ref[level, 0] = field[level, level : level + 2]
        edge_ref[level, 1] = field[level, rows - 2 - level : rows - level]
    acc = None
    for y in range(1, rows - 1):

        def blocks(r, m, half, t, y=y):
            return field[(m + 1) % MOM, y, r, half, t] if m < y < rows - 1 - m else None

        acc = product(acc, blocks, left_ref, y)
    sum_ref[...] = acc


def outer_kernel(lo_ref, hi_ref, pres_ref, left_ref, sum_ref, edge_ref, out_ref, field, presb):
    rows = left_ref.shape[0]
    wraps = wrap_masks()
    T = range(TILES)
    tail = HALO * 16
    base = (-HALO, rows - 2 * HALO)

    for i in range(HALO):
        for side, src, j in ((0, lo_ref, i), (1, hi_ref, 2 * HALO + i)):
            turned = turn_row(src, i * 16)
            for t in T:
                at = i * TILES + t
                row = src[tail + at // SUB, pl.ds(at % SUB, 1), :]
                mask = jnp.broadcast_to(row, (SUB, LANES))
                presb[side, j, t] = mask
                for q in range(4):
                    at = (4 * t + q) * SUB
                    field[0, side, j, q // 2, q % 2, t] = turned[at : at + SUB] * mask
    for side in (0, 1):
        for i in range(HALO):
            j = HALO + i
            for t in T:
                row = pres_ref[base[side] + j, pl.ds(t, 1), :]
                presb[side, j, t] = jnp.broadcast_to(row, (SUB, LANES))

    def given(level, side):
        first = HALO + level if side == 0 else 2 * HALO - 2 - level
        return first, first + 1

    def tile(level, side, j, r, half, t):
        spots = given(level, side)
        if j in spots:
            return edge_ref[level, side, spots.index(j), r, half, t]
        return field[level, side, j, r, half, t]

    def load(level, side, j, half):
        return [[tile(level, side, j, r, half, t) for t in T] for r in (0, 1)]

    for level in range(MOM):
        for side in (0, 1):
            first = 1 + level if side == 0 else 2 * HALO - 1 - level
            for half in (0, 1):
                window = [load(level, side, first + k, half) for k in range(-1, 5)]
                for k in range(4):
                    j = first + k
                    mask = scaled(level, [presb[side, j, t] for t in T])
                    old = load(level - 1, side, j, half) if level > 1 else None
                    values = stencil_row(level, j % 2, *window[k : k + 3], old, mask, wraps)
                    for r in (0, 1):
                        for t in T:
                            field[(level + 1) % MOM, side, j, r, half, t] = values[r][t]

    acc = sum_ref[...]
    for y in [*range(HALO), *range(rows - HALO, rows)]:
        side = 0 if y < HALO else 1

        def blocks(r, m, half, t, y=y, side=side):
            if m < y < rows - 1 - m:
                return None
            return field[(m + 1) % MOM, side, y - base[side], r, half, t]

        acc = product(acc, blocks, left_ref, y)
    half_rows = MOM * 2 * SUB
    top, bottom = acc[:half_rows], acc[half_rows:]
    lane_out = lax.broadcasted_iota(jnp.int32, top.shape, 1)
    out_ref[...] = pltpu.roll(bottom, LANES // 2, 1) + jnp.where(lane_out < LANES // 2, top, -top)


ROW = (2, 2, TILES, SUB, LANES)


def inner_moments(recv, pres, left):
    rows, n2, _ = left.shape
    vm = pl.BlockSpec(memory_space=pltpu.VMEM)
    return pl.pallas_call(
        inner_kernel,
        in_specs=[vm] * 3,
        out_specs=[vm] * 2,
        out_shape=[
            jax.ShapeDtypeStruct((2 * MOM * 2 * SUB, n2), F32),
            jax.ShapeDtypeStruct((MOM, 2, 2, *ROW), F32),
        ],
        scratch_shapes=[
            pltpu.VMEM((MOM, rows, *ROW), F32),
            pltpu.VMEM((rows, TILES, SUB, LANES), F32),
        ],
        compiler_params=pltpu.CompilerParams(vmem_limit_bytes=40 * 2**20),
        cost_estimate=pl.CostEstimate(flops=10**9, bytes_accessed=10**7, transcendentals=0),
        name="inner_moments",
    )(recv, pres, left)


def outer_moments(lo, hi, pres, left, inner_sum, edges):
    n2 = left.shape[1]
    vm = pl.BlockSpec(memory_space=pltpu.VMEM)
    return pl.pallas_call(
        outer_kernel,
        in_specs=[vm] * 6,
        out_specs=vm,
        out_shape=jax.ShapeDtypeStruct((MOM * 2 * SUB, n2), F32),
        scratch_shapes=[
            pltpu.VMEM((MOM, 2, 3 * HALO, *ROW), F32),
            pltpu.VMEM((2, 3 * HALO, TILES, SUB, LANES), F32),
        ],
        compiler_params=pltpu.CompilerParams(vmem_limit_bytes=40 * 2**20),
        name="outer_moments",
    )(lo, hi, pres, left, inner_sum, edges)


def per_device(right_vectors, left_vectors, vacancy):
    parts, width_group, groups, slabs, _, piece = right_vectors.shape
    count = lax.axis_size("sites")
    up = [(i, (i + 1) % count) for i in range(count)]
    down = [((i + 1) % count, i) for i in range(count)]
    n_left, rows, width = left_vectors.shape[1:]

    packed = pack(right_vectors.reshape(parts * width_group, groups, slabs, piece))
    packed, left_vectors = lax.optimization_barrier((packed, left_vectors))
    recv = lax.all_to_all(packed, ("cols", "sites"), 0, 0, tiled=True)

    site = lax.broadcasted_iota(jnp.int32, (width, width), 0)
    place = lax.broadcasted_iota(jnp.int32, (width, width), 1)
    to_place = (site % TILES * LANES + site // TILES == place).astype(jnp.bfloat16)
    left = left_vectors.reshape(2 * n_left * rows, width)
    left = jnp.dot(left, to_place, preferred_element_type=jnp.bfloat16)
    left = jnp.swapaxes(left.reshape(2 * n_left, rows, width), 0, 1)
    present = jnp.dot(vacancy.astype(jnp.bfloat16), to_place, preferred_element_type=F32)
    present = present.reshape(rows, TILES, LANES)
    recv, left, present = lax.optimization_barrier((recv, left, present))

    edge = HALO * width // piece
    low_mask = present[:HALO].reshape(-1, SUB, LANES)
    high_mask = present[rows - HALO :].reshape(-1, SUB, LANES)
    lo = lax.ppermute(jnp.concatenate([recv[recv.shape[0] - edge :], high_mask]), "sites", up)
    hi = lax.ppermute(jnp.concatenate([recv[:edge], low_mask]), "sites", down)
    inner_sum, edges = inner_moments(recv, present, left)
    total = outer_moments(lo, hi, present, left, inner_sum, edges)
    step = 1
    while step < count:
        total = total + lax.ppermute(total, "sites", [(i, i ^ step) for i in range(count)])
        step *= 2
    out = total.reshape(MOM, width_group, 2, n_left)
    return jnp.transpose(out, (2, 0, 3, 1))[..., None]


def solution(mesh):
    return jax.shard_map(
        per_device,
        mesh=mesh,
        in_specs=(
            P(None, None, None, None, ("cols", "sites"), None),
            P(None, None, "sites", None),
            P("sites", None),
        ),
        out_specs=P(None, None, None, None, "cols"),
        check_vma=False,
    )
```

```python
import jax
import jax.numpy as jnp
from jax import lax
from jax.experimental import pallas as pl
from jax.experimental.pallas import tpu as pltpu
from jax.sharding import PartitionSpec as P

MOM = 4
HALO = 4
ONSITE_MASS = 0.3
SECOND_HOP = 0.2
BAND_SCALE = 4.5
LANES = 128
SUB = 8
TILES = 4
F32 = jnp.float32


PACK_GROUPS = 4
MERGES = 16


def pack_kernel(in_ref, out_ref, turned):
    columns, groups, slabs, width = in_ref.shape
    lane = lax.broadcasted_iota(jnp.int32, (SUB, LANES), 1)
    odd, high = lane // width % 2 == 1, lane // width >= 2
    swapped = jnp.where(odd, lane - width, lane + width)
    for k in range(groups):
        for base in range(0, slabs, SUB):
            octets = [
                jnp.swapaxes(in_ref[c : c + SUB, k, base : base + SUB, :], 0, 1)
                for c in range(0, columns, SUB)
            ]
            for half in (0, 4):
                rows = [octet[half + s] for s in range(4) for octet in octets]
                turned[(k * slabs + base + half) // 4] = jnp.concatenate(rows, axis=0).T

    @pl.loop(0, groups * slabs // 4 // MERGES)
    def _(i):
        for j in range(MERGES):
            slot = i * MERGES + j
            v = [turned[slot, pl.ds(t, SUB, stride=TILES), :] for t in range(TILES)]
            for p in (0, 2):
                low, upper = v[p], v[p + 1]
                moved = jnp.take_along_axis(jnp.where(odd, low, upper), swapped, axis=1)
                v[p], v[p + 1] = jnp.where(odd, moved, low), jnp.where(odd, upper, moved)
            for p in (0, 1):
                low, upper = v[p], v[p + 2]
                moved = pltpu.roll(jnp.where(high, low, upper), LANES // 2, 1)
                v[p], v[p + 2] = jnp.where(high, moved, low), jnp.where(high, upper, moved)
            for s in range(4):
                out_ref[slot * 4 // slabs, slot * 4 % slabs + s] = v[s]


def pack(pieces):
    columns, groups, slabs, width = pieces.shape
    step = PACK_GROUPS
    out = pl.pallas_call(
        pack_kernel,
        grid=(groups // step,),
        in_specs=[pl.BlockSpec((columns, step, slabs, width), lambda k: (0, k, 0, 0))],
        out_specs=pl.BlockSpec((step, slabs, SUB, LANES), lambda k: (k, 0, 0, 0)),
        out_shape=jax.ShapeDtypeStruct((groups, slabs, SUB, LANES), F32),
        scratch_shapes=[pltpu.VMEM((step * slabs // 4, width, LANES), F32)],
        name="pack",
    )(pieces)
    return out.reshape(groups * slabs, SUB, LANES)


def wrap_masks():
    lane = lax.broadcasted_iota(jnp.int32, (SUB, LANES), 1)
    return lane == 0, lane == LANES - 1


def ahead(tiles, is_last):
    wrapped = jnp.where(is_last, 0.0, pltpu.roll(tiles[0], LANES - 1, 1))
    return tiles[1:] + [wrapped]


def behind(tiles, is_first):
    wrapped = jnp.where(is_first, 0.0, pltpu.roll(tiles[-1], 1, 1))
    return [wrapped] + tiles[:-1]


def stencil_row(level, parity, below, centre, above, old, mask, wraps):
    is_first, is_last = wraps
    T = range(TILES)
    nxt, prv, second = [], [], []
    for r in (0, 1):
        w = centre[r]
        diag = [above[r][t] + below[r][t] for t in T]
        fore, back = ahead(w, is_last), behind(w, is_first)
        if level == 0:
            a = ahead([2.0 * fore[t] - diag[t] for t in T], is_last)
            b = behind([2.0 * back[t] - diag[t] for t in T], is_first)
            second.append([a[t] + b[t] for t in T])
        else:
            a = ahead([fore[t] - diag[t] for t in T], is_last)
            b = behind([back[t] - diag[t] for t in T], is_first)
            second.append([a[t] - b[t] for t in T])
        nxt.append(fore)
        prv.append(back)
    result = []
    for r in (0, 1):
        values = []
        for t in T:
            sign = 1.0 if (parity + t) % 2 == 0 else -1.0
            if level == 0:
                along = prv[1][t] - nxt[1][t] if r == 0 else nxt[0][t] - prv[0][t]
                total = along - (SECOND_HOP * sign) * second[r][t]
            else:
                vertical = above[r][t] if sign > 0 else below[r][t]
                near = (nxt[r][t] + prv[r][t]) + vertical
                turn = -sign if r == 0 else sign
                total = near + (
                    (ONSITE_MASS * sign) * centre[r][t] + (SECOND_HOP * turn) * second[1 - r][t]
                )
            total = total * mask[t]
            values.append(total - old[r][t] if level > 1 else total)
        result.append(values)
    return result


SCALES = (1.0, 1.0 / BAND_SCALE, 2.0 / BAND_SCALE, 2.0 / BAND_SCALE)


def scaled(level, mask):
    return mask if level == 0 else [SCALES[level] * m for m in mask]


def turn_row(src, first):
    return src[pl.ds(first, 16)].reshape(LANES, LANES).T


def product(acc, blocks, left_ref, y):
    for t in range(TILES):
        zero = jnp.zeros((SUB, LANES), F32)
        stacked = [blocks(r, m, h, t) for r in (0, 1) for m in range(MOM) for h in (0, 1)]
        rhs = jnp.concatenate([zero if b is None else b for b in stacked], axis=0)
        term = lax.dot_general(
            rhs.astype(jnp.bfloat16),
            left_ref[y, :, t * LANES : (t + 1) * LANES],
            (((1,), (1,)), ((), ())),
            preferred_element_type=F32,
        )
        acc = term if acc is None else acc + term
    return acc


def inner_kernel(recv_ref, pres_ref, left_ref, sum_ref, edge_ref, field, presb):
    rows = left_ref.shape[0]
    wraps = wrap_masks()
    T = range(TILES)

    @pl.loop(0, rows // 4)
    def _(i):
        for k in range(4):
            y = 4 * i + k
            turned = turn_row(recv_ref, y * 16)
            for t in T:
                mask = jnp.broadcast_to(pres_ref[y, pl.ds(t, 1), :], (SUB, LANES))
                presb[y, t] = mask
                for q in range(4):
                    at = (4 * t + q) * SUB
                    field[0, y, q // 2, q % 2, t] = turned[at : at + SUB] * mask

    def load(level, y, half):
        return [[field[level, y, r, half, t] for t in T] for r in (0, 1)]

    for level in range(MOM):
        first = level + 1

        @pl.loop(0, (rows - 2 * first) // 2)
        def _(i, level=level, first=first):
            y = first + 2 * i
            masks = [scaled(level, [presb[y + k, t] for t in T]) for k in (0, 1)]
            for half in (0, 1):
                window = [load(level, y + k, half) for k in (-1, 0, 1, 2)]
                for k in (0, 1):
                    old = load(level - 1, y + k, half) if level > 1 else None
                    values = stencil_row(
                        level, (first + k) % 2, *window[k : k + 3], old, masks[k], wraps
                    )
                    for r in (0, 1):
                        for t in T:
                            field[(level + 1) % MOM, y + k, r, half, t] = values[r][t]

    for level in range(MOM):
        edge_ref[level, 0] = field[level, level : level + 2]
        edge_ref[level, 1] = field[level, rows - 2 - level : rows - level]
    acc = None
    for y in range(1, rows - 1):

        def blocks(r, m, half, t, y=y):
            return field[(m + 1) % MOM, y, r, half, t] if m < y < rows - 1 - m else None

        acc = product(acc, blocks, left_ref, y)
    sum_ref[...] = acc


def outer_kernel(lo_ref, hi_ref, pres_ref, left_ref, sum_ref, edge_ref, out_ref, field, presb):
    rows = left_ref.shape[0]
    wraps = wrap_masks()
    T = range(TILES)
    tail = HALO * 16
    base = (-HALO, rows - 2 * HALO)

    for i in range(HALO):
        for side, src, j in ((0, lo_ref, i), (1, hi_ref, 2 * HALO + i)):
            turned = turn_row(src, i * 16)
            for t in T:
                at = i * TILES + t
                row = src[tail + at // SUB, pl.ds(at % SUB, 1), :]
                mask = jnp.broadcast_to(row, (SUB, LANES))
                presb[side, j, t] = mask
                for q in range(4):
                    at = (4 * t + q) * SUB
                    field[0, side, j, q // 2, q % 2, t] = turned[at : at + SUB] * mask
    for side in (0, 1):
        for i in range(HALO):
            j = HALO + i
            for t in T:
                row = pres_ref[base[side] + j, pl.ds(t, 1), :]
                presb[side, j, t] = jnp.broadcast_to(row, (SUB, LANES))

    def given(level, side):
        first = HALO + level if side == 0 else 2 * HALO - 2 - level
        return first, first + 1

    def tile(level, side, j, r, half, t):
        spots = given(level, side)
        if j in spots:
            return edge_ref[level, side, spots.index(j), r, half, t]
        return field[level, side, j, r, half, t]

    def load(level, side, j, half):
        return [[tile(level, side, j, r, half, t) for t in T] for r in (0, 1)]

    for level in range(MOM):
        for side in (0, 1):
            first = 1 + level if side == 0 else 2 * HALO - 1 - level
            for half in (0, 1):
                window = [load(level, side, first + k, half) for k in range(-1, 5)]
                for k in range(4):
                    j = first + k
                    mask = scaled(level, [presb[side, j, t] for t in T])
                    old = load(level - 1, side, j, half) if level > 1 else None
                    values = stencil_row(level, j % 2, *window[k : k + 3], old, mask, wraps)
                    for r in (0, 1):
                        for t in T:
                            field[(level + 1) % MOM, side, j, r, half, t] = values[r][t]

    acc = sum_ref[...]
    for y in [*range(HALO), *range(rows - HALO, rows)]:
        side = 0 if y < HALO else 1

        def blocks(r, m, half, t, y=y, side=side):
            if m < y < rows - 1 - m:
                return None
            return field[(m + 1) % MOM, side, y - base[side], r, half, t]

        acc = product(acc, blocks, left_ref, y)
    half_rows = MOM * 2 * SUB
    top, bottom = acc[:half_rows], acc[half_rows:]
    lane_out = lax.broadcasted_iota(jnp.int32, top.shape, 1)
    out_ref[...] = pltpu.roll(bottom, LANES // 2, 1) + jnp.where(lane_out < LANES // 2, top, -top)


ROW = (2, 2, TILES, SUB, LANES)


def inner_moments(recv, pres, left):
    rows, n2, _ = left.shape
    vm = pl.BlockSpec(memory_space=pltpu.VMEM)
    return pl.pallas_call(
        inner_kernel,
        in_specs=[vm] * 3,
        out_specs=[vm] * 2,
        out_shape=[
            jax.ShapeDtypeStruct((2 * MOM * 2 * SUB, n2), F32),
            jax.ShapeDtypeStruct((MOM, 2, 2, *ROW), F32),
        ],
        scratch_shapes=[
            pltpu.VMEM((MOM, rows, *ROW), F32),
            pltpu.VMEM((rows, TILES, SUB, LANES), F32),
        ],
        compiler_params=pltpu.CompilerParams(vmem_limit_bytes=40 * 2**20),
        cost_estimate=pl.CostEstimate(flops=10**9, bytes_accessed=10**7, transcendentals=0),
        name="inner_moments",
    )(recv, pres, left)


def outer_moments(lo, hi, pres, left, inner_sum, edges):
    n2 = left.shape[1]
    vm = pl.BlockSpec(memory_space=pltpu.VMEM)
    return pl.pallas_call(
        outer_kernel,
        in_specs=[vm] * 6,
        out_specs=vm,
        out_shape=jax.ShapeDtypeStruct((MOM * 2 * SUB, n2), F32),
        scratch_shapes=[
            pltpu.VMEM((MOM, 2, 3 * HALO, *ROW), F32),
            pltpu.VMEM((2, 3 * HALO, TILES, SUB, LANES), F32),
        ],
        compiler_params=pltpu.CompilerParams(vmem_limit_bytes=40 * 2**20),
        name="outer_moments",
    )(lo, hi, pres, left, inner_sum, edges)


def per_device(right_vectors, left_vectors, vacancy):
    parts, width_group, groups, slabs, _, piece = right_vectors.shape
    count = lax.axis_size("sites")
    up = [(i, (i + 1) % count) for i in range(count)]
    down = [((i + 1) % count, i) for i in range(count)]
    n_left, rows, width = left_vectors.shape[1:]

    packed = pack(right_vectors.reshape(parts * width_group, groups, slabs, piece))
    packed, left_vectors = lax.optimization_barrier((packed, left_vectors))
    recv = lax.all_to_all(packed, ("cols", "sites"), 0, 0, tiled=True)

    site = lax.broadcasted_iota(jnp.int32, (width, width), 0)
    place = lax.broadcasted_iota(jnp.int32, (width, width), 1)
    to_place = (site % TILES * LANES + site // TILES == place).astype(jnp.bfloat16)
    left = left_vectors.reshape(2 * n_left * rows, width)
    left = jnp.dot(left, to_place, preferred_element_type=jnp.bfloat16)
    left = jnp.swapaxes(left.reshape(2 * n_left, rows, width), 0, 1)
    present = jnp.dot(vacancy.astype(jnp.bfloat16), to_place, preferred_element_type=F32)
    present = present.reshape(rows, TILES, LANES)
    recv, left, present = lax.optimization_barrier((recv, left, present))

    edge = HALO * width // piece
    low_mask = present[:HALO].reshape(-1, SUB, LANES)
    high_mask = present[rows - HALO :].reshape(-1, SUB, LANES)
    lo = lax.ppermute(jnp.concatenate([recv[recv.shape[0] - edge :], high_mask]), "sites", up)
    hi = lax.ppermute(jnp.concatenate([recv[:edge], low_mask]), "sites", down)
    inner_sum, edges = inner_moments(recv, present, left)
    total = outer_moments(lo, hi, present, left, inner_sum, edges)
    for flip in (1, 2, 4, 8, 24):
        total = total + lax.ppermute(total, "sites", [(i, i ^ flip) for i in range(count)])
    out = jnp.stack([total[:, :n_left], total[:, n_left:]]).reshape(2, MOM, width_group, n_left)
    return jnp.swapaxes(out, 2, 3)[..., None]


def solution(mesh):
    return jax.shard_map(
        per_device,
        mesh=mesh,
        in_specs=(
            P(None, None, None, None, ("cols", "sites"), None),
            P(None, None, "sites", None),
            P("sites", None),
        ),
        out_specs=P(None, None, None, None, "cols"),
        check_vma=False,
    )
```

```python
import jax
import jax.numpy as jnp
from jax import lax
from jax.experimental import pallas as pl
from jax.experimental.pallas import tpu as pltpu
from jax.sharding import PartitionSpec as P

MOM = 4
HALO = 4
ONSITE_MASS = 0.3
SECOND_HOP = 0.2
BAND_SCALE = 4.5
LANES = 128
SUB = 8
TILES = 4
F32 = jnp.float32


PACK_GROUPS = 4
MERGES = 16


def pack_kernel(in_ref, out_ref, turned):
    columns, groups, slabs, width = in_ref.shape
    lane = lax.broadcasted_iota(jnp.int32, (SUB, LANES), 1)
    odd, high = lane // width % 2 == 1, lane // width >= 2
    swapped = jnp.where(odd, lane - width, lane + width)
    for k in range(groups):
        for base in range(0, slabs, SUB):
            octets = [
                jnp.swapaxes(in_ref[c : c + SUB, k, base : base + SUB, :], 0, 1)
                for c in range(0, columns, SUB)
            ]
            for half in (0, 4):
                rows = [octet[half + s] for s in range(4) for octet in octets]
                turned[(k * slabs + base + half) // 4] = jnp.concatenate(rows, axis=0).T

    @pl.loop(0, groups * slabs // 4 // MERGES)
    def _(i):
        for j in range(MERGES):
            slot = i * MERGES + j
            v = [turned[slot, pl.ds(t, SUB, stride=TILES), :] for t in range(TILES)]
            for p in (0, 2):
                low, upper = v[p], v[p + 1]
                moved = jnp.take_along_axis(jnp.where(odd, low, upper), swapped, axis=1)
                v[p], v[p + 1] = jnp.where(odd, moved, low), jnp.where(odd, upper, moved)
            for p in (0, 1):
                low, upper = v[p], v[p + 2]
                moved = pltpu.roll(jnp.where(high, low, upper), LANES // 2, 1)
                v[p], v[p + 2] = jnp.where(high, moved, low), jnp.where(high, upper, moved)
            for s in range(4):
                out_ref[slot * 4 // slabs, slot * 4 % slabs + s] = v[s]


def pack(pieces):
    columns, groups, slabs, width = pieces.shape
    step = PACK_GROUPS
    out = pl.pallas_call(
        pack_kernel,
        grid=(groups // step,),
        in_specs=[pl.BlockSpec((columns, step, slabs, width), lambda k: (0, k, 0, 0))],
        out_specs=pl.BlockSpec((step, slabs, SUB, LANES), lambda k: (k, 0, 0, 0)),
        out_shape=jax.ShapeDtypeStruct((groups, slabs, SUB, LANES), F32),
        scratch_shapes=[pltpu.VMEM((step * slabs // 4, width, LANES), F32)],
        name="pack",
    )(pieces)
    return out.reshape(groups * slabs, SUB, LANES)


def wrap_masks():
    lane = lax.broadcasted_iota(jnp.int32, (SUB, LANES), 1)
    return lane == 0, lane == LANES - 1


def ahead(tiles, is_last):
    wrapped = jnp.where(is_last, 0.0, pltpu.roll(tiles[0], LANES - 1, 1))
    return tiles[1:] + [wrapped]


def behind(tiles, is_first):
    wrapped = jnp.where(is_first, 0.0, pltpu.roll(tiles[-1], 1, 1))
    return [wrapped] + tiles[:-1]


def stencil_row(level, parity, below, centre, above, old, mask, wraps):
    is_first, is_last = wraps
    T = range(TILES)
    nxt, prv, second = [], [], []
    for r in (0, 1):
        w = centre[r]
        diag = [above[r][t] + below[r][t] for t in T]
        fore, back = ahead(w, is_last), behind(w, is_first)
        if level == 0:
            a = ahead([2.0 * fore[t] - diag[t] for t in T], is_last)
            b = behind([2.0 * back[t] - diag[t] for t in T], is_first)
            second.append([a[t] + b[t] for t in T])
        else:
            a = ahead([fore[t] - diag[t] for t in T], is_last)
            b = behind([back[t] - diag[t] for t in T], is_first)
            second.append([a[t] - b[t] for t in T])
        nxt.append(fore)
        prv.append(back)
    result = []
    for r in (0, 1):
        values = []
        for t in T:
            sign = 1.0 if (parity + t) % 2 == 0 else -1.0
            if level == 0:
                along = prv[1][t] - nxt[1][t] if r == 0 else nxt[0][t] - prv[0][t]
                total = along - (SECOND_HOP * sign) * second[r][t]
            else:
                vertical = above[r][t] if sign > 0 else below[r][t]
                near = (nxt[r][t] + prv[r][t]) + vertical
                turn = -sign if r == 0 else sign
                total = near + (
                    (ONSITE_MASS * sign) * centre[r][t] + (SECOND_HOP * turn) * second[1 - r][t]
                )
            total = total * mask[t]
            values.append(total - old[r][t] if level > 1 else total)
        result.append(values)
    return result


SCALES = (1.0, 1.0 / BAND_SCALE, 2.0 / BAND_SCALE, 2.0 / BAND_SCALE)


def scaled(level, mask):
    return mask if level == 0 else [SCALES[level] * m for m in mask]


def turn_row(src, first):
    return src[pl.ds(first, 16)].reshape(LANES, LANES).T


def product(acc, blocks, left_ref, y):
    for t in range(TILES):
        zero = jnp.zeros((SUB, LANES), F32)
        stacked = [blocks(r, m, h, t) for r in (0, 1) for m in range(MOM) for h in (0, 1)]
        rhs = jnp.concatenate([zero if b is None else b for b in stacked], axis=0)
        term = lax.dot_general(
            rhs.astype(jnp.bfloat16),
            left_ref[y, :, t * LANES : (t + 1) * LANES],
            (((1,), (1,)), ((), ())),
            preferred_element_type=F32,
        )
        acc = term if acc is None else acc + term
    return acc


def inner_kernel(recv_ref, pres_ref, left_ref, sum_ref, edge_ref, field, presb):
    rows = left_ref.shape[0]
    wraps = wrap_masks()
    T = range(TILES)

    @pl.loop(0, rows // 4)
    def _(i):
        for k in range(4):
            y = 4 * i + k
            turned = turn_row(recv_ref, y * 16)
            for t in T:
                mask = jnp.broadcast_to(pres_ref[y, pl.ds(t, 1), :], (SUB, LANES))
                presb[y, t] = mask
                for q in range(4):
                    at = (4 * t + q) * SUB
                    field[0, y, q // 2, q % 2, t] = turned[at : at + SUB] * mask

    def load(level, y, half):
        return [[field[level, y, r, half, t] for t in T] for r in (0, 1)]

    for level in range(MOM):
        first = level + 1

        @pl.loop(0, (rows - 2 * first) // 2)
        def _(i, level=level, first=first):
            y = first + 2 * i
            masks = [scaled(level, [presb[y + k, t] for t in T]) for k in (0, 1)]
            for half in (0, 1):
                window = [load(level, y + k, half) for k in (-1, 0, 1, 2)]
                for k in (0, 1):
                    old = load(level - 1, y + k, half) if level > 1 else None
                    values = stencil_row(
                        level, (first + k) % 2, *window[k : k + 3], old, masks[k], wraps
                    )
                    for r in (0, 1):
                        for t in T:
                            field[(level + 1) % MOM, y + k, r, half, t] = values[r][t]

    for level in range(MOM):
        edge_ref[level, 0] = field[level, level : level + 2]
        edge_ref[level, 1] = field[level, rows - 2 - level : rows - level]
    acc = None
    for y in range(1, rows - 1):

        def blocks(r, m, half, t, y=y):
            return field[(m + 1) % MOM, y, r, half, t] if m < y < rows - 1 - m else None

        acc = product(acc, blocks, left_ref, y)
    sum_ref[...] = acc


def outer_kernel(lo_ref, hi_ref, pres_ref, left_ref, sum_ref, edge_ref, out_ref, field, presb):
    rows = left_ref.shape[0]
    wraps = wrap_masks()
    T = range(TILES)
    tail = HALO * 16
    base = (-HALO, rows - 2 * HALO)

    for i in range(HALO):
        for side, src, j in ((0, lo_ref, i), (1, hi_ref, 2 * HALO + i)):
            turned = turn_row(src, i * 16)
            for t in T:
                at = i * TILES + t
                row = src[tail + at // SUB, pl.ds(at % SUB, 1), :]
                mask = jnp.broadcast_to(row, (SUB, LANES))
                presb[side, j, t] = mask
                for q in range(4):
                    at = (4 * t + q) * SUB
                    field[0, side, j, q // 2, q % 2, t] = turned[at : at + SUB] * mask
    for side in (0, 1):
        for i in range(HALO):
            j = HALO + i
            for t in T:
                row = pres_ref[base[side] + j, pl.ds(t, 1), :]
                presb[side, j, t] = jnp.broadcast_to(row, (SUB, LANES))

    def given(level, side):
        first = HALO + level if side == 0 else 2 * HALO - 2 - level
        return first, first + 1

    def tile(level, side, j, r, half, t):
        spots = given(level, side)
        if j in spots:
            return edge_ref[level, side, spots.index(j), r, half, t]
        return field[level, side, j, r, half, t]

    def load(level, side, j, half):
        return [[tile(level, side, j, r, half, t) for t in T] for r in (0, 1)]

    for level in range(MOM):
        for side in (0, 1):
            first = 1 + level if side == 0 else 2 * HALO - 1 - level
            for half in (0, 1):
                window = [load(level, side, first + k, half) for k in range(-1, 5)]
                for k in range(4):
                    j = first + k
                    mask = scaled(level, [presb[side, j, t] for t in T])
                    old = load(level - 1, side, j, half) if level > 1 else None
                    values = stencil_row(level, j % 2, *window[k : k + 3], old, mask, wraps)
                    for r in (0, 1):
                        for t in T:
                            field[(level + 1) % MOM, side, j, r, half, t] = values[r][t]

    acc = sum_ref[...]
    for y in [*range(HALO), *range(rows - HALO, rows)]:
        side = 0 if y < HALO else 1

        def blocks(r, m, half, t, y=y, side=side):
            if m < y < rows - 1 - m:
                return None
            return field[(m + 1) % MOM, side, y - base[side], r, half, t]

        acc = product(acc, blocks, left_ref, y)
    half_rows = MOM * 2 * SUB
    top, bottom = acc[:half_rows], acc[half_rows:]
    lane_out = lax.broadcasted_iota(jnp.int32, top.shape, 1)
    out_ref[...] = pltpu.roll(bottom, LANES // 2, 1) + jnp.where(lane_out < LANES // 2, top, -top)


ROW = (2, 2, TILES, SUB, LANES)


def inner_moments(recv, pres, left):
    rows, n2, _ = left.shape
    vm = pl.BlockSpec(memory_space=pltpu.VMEM)
    return pl.pallas_call(
        inner_kernel,
        in_specs=[vm] * 3,
        out_specs=[vm] * 2,
        out_shape=[
            jax.ShapeDtypeStruct((2 * MOM * 2 * SUB, n2), F32),
            jax.ShapeDtypeStruct((MOM, 2, 2, *ROW), F32),
        ],
        scratch_shapes=[
            pltpu.VMEM((MOM, rows, *ROW), F32),
            pltpu.VMEM((rows, TILES, SUB, LANES), F32),
        ],
        compiler_params=pltpu.CompilerParams(vmem_limit_bytes=40 * 2**20),
        cost_estimate=pl.CostEstimate(flops=10**9, bytes_accessed=10**7, transcendentals=0),
        name="inner_moments",
    )(recv, pres, left)


def outer_moments(lo, hi, pres, left, inner_sum, edges):
    n2 = left.shape[1]
    vm = pl.BlockSpec(memory_space=pltpu.VMEM)
    return pl.pallas_call(
        outer_kernel,
        in_specs=[vm] * 6,
        out_specs=vm,
        out_shape=jax.ShapeDtypeStruct((MOM * 2 * SUB, n2), F32),
        scratch_shapes=[
            pltpu.VMEM((MOM, 2, 3 * HALO, *ROW), F32),
            pltpu.VMEM((2, 3 * HALO, TILES, SUB, LANES), F32),
        ],
        compiler_params=pltpu.CompilerParams(vmem_limit_bytes=40 * 2**20),
        name="outer_moments",
    )(lo, hi, pres, left, inner_sum, edges)


def per_device(right_vectors, left_vectors, vacancy):
    parts, width_group, groups, slabs, _, piece = right_vectors.shape
    count = lax.axis_size("sites")
    up = [(i, (i + 1) % count) for i in range(count)]
    down = [((i + 1) % count, i) for i in range(count)]
    n_left, rows, width = left_vectors.shape[1:]

    packed = pack(right_vectors.reshape(parts * width_group, groups, slabs, piece))
    packed, left_vectors = lax.optimization_barrier((packed, left_vectors))
    recv = lax.all_to_all(packed, ("cols", "sites"), 0, 0, tiled=True)

    site = lax.broadcasted_iota(jnp.int32, (width, width), 0)
    place = lax.broadcasted_iota(jnp.int32, (width, width), 1)
    to_place = (site % TILES * LANES + site // TILES == place).astype(jnp.bfloat16)
    left = left_vectors.reshape(2 * n_left * rows, width)
    left = jnp.dot(left, to_place, preferred_element_type=jnp.bfloat16)
    left = jnp.swapaxes(left.reshape(2 * n_left, rows, width), 0, 1)
    present = jnp.dot(vacancy.astype(jnp.bfloat16), to_place, preferred_element_type=F32)
    present = present.reshape(rows, TILES, LANES)
    recv, left, present = lax.optimization_barrier((recv, left, present))

    edge = HALO * width // piece
    low_mask = present[:HALO].reshape(-1, SUB, LANES)
    high_mask = present[rows - HALO :].reshape(-1, SUB, LANES)
    lo = lax.ppermute(jnp.concatenate([recv[recv.shape[0] - edge :], high_mask]), "sites", up)
    hi = lax.ppermute(jnp.concatenate([recv[:edge], low_mask]), "sites", down)
    inner_sum, edges = inner_moments(recv, present, left)
    total = outer_moments(lo, hi, present, left, inner_sum, edges)
    def moved(values, target):
        return lax.ppermute(values, "sites", [(i, target(i)) for i in range(count)])

    for flip in (1, 2, 4):
        total = total + moved(total, lambda i: i ^ flip)
    far, one, other = [moved(total, lambda i: (i + 8 * k) % count) for k in (2, 1, 3)]
    total = (total + far) + (one + other)
    out = jnp.stack([total[:, :n_left], total[:, n_left:]]).reshape(2, MOM, width_group, n_left)
    return jnp.swapaxes(out, 2, 3)[..., None]


def solution(mesh):
    return jax.shard_map(
        per_device,
        mesh=mesh,
        in_specs=(
            P(None, None, None, None, ("cols", "sites"), None),
            P(None, None, "sites", None),
            P("sites", None),
        ),
        out_specs=P(None, None, None, None, "cols"),
        check_vma=False,
    )
```

```python
import functools

import jax
import jax.numpy as jnp
from jax import lax
from jax.experimental import pallas as pl
from jax.experimental.pallas import tpu as pltpu
from jax.sharding import PartitionSpec as P

MOM = 4
HALO = 4
ONSITE_MASS = 0.3
SECOND_HOP = 0.2
BAND_SCALE = 4.5
LANES = 128
SUB = 8
TILES = 4
F32 = jnp.float32


PACK_GROUPS = 4
MERGES = 16


def pack_kernel(in_ref, out_ref, turned):
    columns, groups, slabs, width = in_ref.shape
    lane = lax.broadcasted_iota(jnp.int32, (SUB, LANES), 1)
    odd, high = lane // width % 2 == 1, lane // width >= 2
    swapped = jnp.where(odd, lane - width, lane + width)
    for k in range(groups):
        for base in range(0, slabs, SUB):
            octets = [
                jnp.swapaxes(in_ref[c : c + SUB, k, base : base + SUB, :], 0, 1)
                for c in range(0, columns, SUB)
            ]
            for half in (0, 4):
                rows = [octet[half + s] for s in range(4) for octet in octets]
                turned[(k * slabs + base + half) // 4] = jnp.concatenate(rows, axis=0).T

    @pl.loop(0, groups * slabs // 4 // MERGES)
    def _(i):
        for j in range(MERGES):
            slot = i * MERGES + j
            v = [turned[slot, pl.ds(t, SUB, stride=TILES), :] for t in range(TILES)]
            for p in (0, 2):
                low, upper = v[p], v[p + 1]
                moved = jnp.take_along_axis(jnp.where(odd, low, upper), swapped, axis=1)
                v[p], v[p + 1] = jnp.where(odd, moved, low), jnp.where(odd, upper, moved)
            for p in (0, 1):
                low, upper = v[p], v[p + 2]
                moved = pltpu.roll(jnp.where(high, low, upper), LANES // 2, 1)
                v[p], v[p + 2] = jnp.where(high, moved, low), jnp.where(high, upper, moved)
            for s in range(4):
                out_ref[slot * 4 // slabs, slot * 4 % slabs + s] = v[s]


def pack(pieces):
    columns, groups, slabs, width = pieces.shape
    step = PACK_GROUPS
    out = pl.pallas_call(
        pack_kernel,
        grid=(groups // step,),
        in_specs=[pl.BlockSpec((columns, step, slabs, width), lambda k: (0, k, 0, 0))],
        out_specs=pl.BlockSpec((step, slabs, SUB, LANES), lambda k: (k, 0, 0, 0)),
        out_shape=jax.ShapeDtypeStruct((groups, slabs, SUB, LANES), F32),
        scratch_shapes=[pltpu.VMEM((step * slabs // 4, width, LANES), F32)],
        name="pack",
    )(pieces)
    return out.reshape(groups * slabs, SUB, LANES)


def wrap_masks():
    lane = lax.broadcasted_iota(jnp.int32, (SUB, LANES), 1)
    return lane == 0, lane == LANES - 1


def ahead(tiles, is_last):
    wrapped = jnp.where(is_last, 0.0, pltpu.roll(tiles[0], LANES - 1, 1))
    return tiles[1:] + [wrapped]


def behind(tiles, is_first):
    wrapped = jnp.where(is_first, 0.0, pltpu.roll(tiles[-1], 1, 1))
    return [wrapped] + tiles[:-1]


def stencil_row(level, parity, below, centre, above, old, mask, wraps):
    is_first, is_last = wraps
    T = range(TILES)
    nxt, prv, second = [], [], []
    for r in (0, 1):
        w = centre[r]
        diag = [above[r][t] + below[r][t] for t in T]
        fore, back = ahead(w, is_last), behind(w, is_first)
        if level == 0:
            a = ahead([2.0 * fore[t] - diag[t] for t in T], is_last)
            b = behind([2.0 * back[t] - diag[t] for t in T], is_first)
            second.append([a[t] + b[t] for t in T])
        else:
            a = ahead([fore[t] - diag[t] for t in T], is_last)
            b = behind([back[t] - diag[t] for t in T], is_first)
            second.append([a[t] - b[t] for t in T])
        nxt.append(fore)
        prv.append(back)
    result = []
    for r in (0, 1):
        values = []
        for t in T:
            sign = 1.0 if (parity + t) % 2 == 0 else -1.0
            if level == 0:
                along = prv[1][t] - nxt[1][t] if r == 0 else nxt[0][t] - prv[0][t]
                total = along - (SECOND_HOP * sign) * second[r][t]
            else:
                vertical = above[r][t] if sign > 0 else below[r][t]
                near = (nxt[r][t] + prv[r][t]) + vertical
                turn = -sign if r == 0 else sign
                total = near + (
                    (ONSITE_MASS * sign) * centre[r][t] + (SECOND_HOP * turn) * second[1 - r][t]
                )
            total = total * mask[t]
            values.append(total - old[r][t] if level > 1 else total)
        result.append(values)
    return result


SCALES = (1.0, 1.0 / BAND_SCALE, 2.0 / BAND_SCALE, 2.0 / BAND_SCALE)


def scaled(level, mask):
    return mask if level == 0 else [SCALES[level] * m for m in mask]


def turn_row(src, first):
    return src[pl.ds(first, 16)].reshape(LANES, LANES).T


def product(acc, blocks, left_ref, y):
    for t in range(TILES):
        zero = jnp.zeros((SUB, LANES), F32)
        stacked = [blocks(r, m, h, t) for r in (0, 1) for m in range(MOM) for h in (0, 1)]
        rhs = jnp.concatenate([zero if b is None else b for b in stacked], axis=0)
        term = lax.dot_general(
            rhs.astype(jnp.bfloat16),
            left_ref[y, :, t * LANES : (t + 1) * LANES],
            (((1,), (1,)), ((), ())),
            preferred_element_type=F32,
        )
        acc = term if acc is None else acc + term
    return acc


def inner_kernel(recv_ref, pres_ref, left_ref, sum_ref, edge_ref, field, presb):
    rows = left_ref.shape[0]
    wraps = wrap_masks()
    T = range(TILES)

    @pl.loop(0, rows // 4)
    def _(i):
        for k in range(4):
            y = 4 * i + k
            turned = turn_row(recv_ref, y * 16)
            for t in T:
                mask = jnp.broadcast_to(pres_ref[y, pl.ds(t, 1), :], (SUB, LANES))
                presb[y, t] = mask
                for q in range(4):
                    at = (4 * t + q) * SUB
                    field[0, y, q // 2, q % 2, t] = turned[at : at + SUB] * mask

    def load(level, y, half):
        return [[field[level, y, r, half, t] for t in T] for r in (0, 1)]

    for level in range(MOM):
        first = level + 1

        @pl.loop(0, (rows - 2 * first) // 2)
        def _(i, level=level, first=first):
            y = first + 2 * i
            masks = [scaled(level, [presb[y + k, t] for t in T]) for k in (0, 1)]
            for half in (0, 1):
                window = [load(level, y + k, half) for k in (-1, 0, 1, 2)]
                for k in (0, 1):
                    old = load(level - 1, y + k, half) if level > 1 else None
                    values = stencil_row(
                        level, (first + k) % 2, *window[k : k + 3], old, masks[k], wraps
                    )
                    for r in (0, 1):
                        for t in T:
                            field[(level + 1) % MOM, y + k, r, half, t] = values[r][t]

    for level in range(MOM):
        edge_ref[level, 0] = field[level, level : level + 2]
        edge_ref[level, 1] = field[level, rows - 2 - level : rows - level]
    acc = None
    for y in range(1, rows - 1):

        def blocks(r, m, half, t, y=y):
            return field[(m + 1) % MOM, y, r, half, t] if m < y < rows - 1 - m else None

        acc = product(acc, blocks, left_ref, y)
    sum_ref[...] = acc


def edge_kernel(across, core_ref, src_ref, pres_ref, left_ref, sum_ref, edge_ref, out_ref, field, presb):
    rows = left_ref.shape[0]
    wraps = wrap_masks()
    T = range(TILES)
    tail = HALO * 16

    def side_sum(side):
        base = (-HALO, rows - 2 * HALO)[side]
        for i in range(HALO):
            j = i if side == 0 else 2 * HALO + i
            turned = turn_row(src_ref, i * 16)
            for t in T:
                at = i * TILES + t
                row = src_ref[tail + at // SUB, pl.ds(at % SUB, 1), :]
                mask = jnp.broadcast_to(row, (SUB, LANES))
                presb[j, t] = mask
                for q in range(4):
                    at = (4 * t + q) * SUB
                    field[0, j, q // 2, q % 2, t] = turned[at : at + SUB] * mask
        for j in range(HALO, 2 * HALO):
            for t in T:
                presb[j, t] = jnp.broadcast_to(pres_ref[base + j, pl.ds(t, 1), :], (SUB, LANES))

        def tile(level, j, r, half, t):
            first = HALO + level if side == 0 else 2 * HALO - 2 - level
            if first <= j < first + 2:
                return edge_ref[level, side, j - first, r, half, t]
            return field[level, j, r, half, t]

        def load(level, j, half):
            return [[tile(level, j, r, half, t) for t in T] for r in (0, 1)]

        for level in range(MOM):
            first = 1 + level if side == 0 else 2 * HALO - 1 - level
            for half in (0, 1):
                window = [load(level, first + k, half) for k in range(-1, 5)]
                for k in range(4):
                    j = first + k
                    mask = scaled(level, [presb[j, t] for t in T])
                    old = load(level - 1, j, half) if level > 1 else None
                    values = stencil_row(level, j % 2, *window[k : k + 3], old, mask, wraps)
                    for r in (0, 1):
                        for t in T:
                            field[(level + 1) % MOM, j, r, half, t] = values[r][t]

        acc = sum_ref[...]
        for y in range(HALO) if side == 0 else range(rows - HALO, rows):

            def blocks(r, m, half, t, y=y):
                if m < y < rows - 1 - m:
                    return None
                return field[(m + 1) % MOM, y - base, r, half, t]

            acc = product(acc, blocks, left_ref, y)
        if across:
            half_rows = MOM * 2 * SUB
            top, bottom = acc[:half_rows], acc[half_rows:]
            lane_out = lax.broadcasted_iota(jnp.int32, top.shape, 1)
            acc = pltpu.roll(bottom, LANES // 2, 1) + jnp.where(lane_out < LANES // 2, top, -top)
        out_ref[...] = acc

    for core in (0, 1):

        @pl.when(core_ref[0] == core)
        def _(side=core if across else 1 - core):
            side_sum(side)


ROW = (2, 2, TILES, SUB, LANES)


def inner_moments(recv, pres, left):
    rows, n2, _ = left.shape
    vm = pl.BlockSpec(memory_space=pltpu.VMEM)
    return pl.pallas_call(
        inner_kernel,
        in_specs=[vm] * 3,
        out_specs=[vm] * 2,
        out_shape=[
            jax.ShapeDtypeStruct((2 * MOM * 2 * SUB, n2), F32),
            jax.ShapeDtypeStruct((MOM, 2, 2, *ROW), F32),
        ],
        scratch_shapes=[
            pltpu.VMEM((MOM, rows, *ROW), F32),
            pltpu.VMEM((rows, TILES, SUB, LANES), F32),
        ],
        compiler_params=pltpu.CompilerParams(vmem_limit_bytes=40 * 2**20),
        cost_estimate=pl.CostEstimate(flops=10**9, bytes_accessed=10**7, transcendentals=0),
        name="inner_moments",
    )(recv, pres, left)


def edge_moments(across, core, src, pres, left, total, edges):
    n2 = left.shape[1]
    vm = pl.BlockSpec(memory_space=pltpu.VMEM)
    return pl.pallas_call(
        functools.partial(edge_kernel, across),
        in_specs=[pl.BlockSpec(memory_space=pltpu.SMEM)] + [vm] * 5,
        out_specs=vm,
        out_shape=jax.ShapeDtypeStruct(((1 if across else 2) * MOM * 2 * SUB, n2), F32),
        scratch_shapes=[
            pltpu.VMEM((MOM, 3 * HALO, *ROW), F32),
            pltpu.VMEM((3 * HALO, TILES, SUB, LANES), F32),
        ],
        compiler_params=pltpu.CompilerParams(vmem_limit_bytes=40 * 2**20),
        cost_estimate=pl.CostEstimate(flops=10**8, bytes_accessed=10**6, transcendentals=0),
        name="edge_across" if across else "edge_sibling",
    )(core, src, pres, left, total, edges)


def per_device(right_vectors, left_vectors, vacancy):
    parts, width_group, groups, slabs, _, piece = right_vectors.shape
    count = lax.axis_size("sites")
    n_left, rows, width = left_vectors.shape[1:]

    packed = pack(right_vectors.reshape(parts * width_group, groups, slabs, piece))
    packed, left_vectors = lax.optimization_barrier((packed, left_vectors))
    recv = lax.all_to_all(packed, ("cols", "sites"), 0, 0, tiled=True)

    site = lax.broadcasted_iota(jnp.int32, (width, width), 0)
    place = lax.broadcasted_iota(jnp.int32, (width, width), 1)
    to_place = (site % TILES * LANES + site // TILES == place).astype(jnp.bfloat16)
    left = left_vectors.reshape(2 * n_left * rows, width)
    left = jnp.dot(left, to_place, preferred_element_type=jnp.bfloat16)
    left = jnp.swapaxes(left.reshape(2 * n_left, rows, width), 0, 1)
    present = jnp.dot(vacancy.astype(jnp.bfloat16), to_place, preferred_element_type=F32)
    present = present.reshape(rows, TILES, LANES)
    recv, left, present = lax.optimization_barrier((recv, left, present))

    edge = HALO * width // piece
    low_mask = present[:HALO].reshape(-1, SUB, LANES)
    high_mask = present[rows - HALO :].reshape(-1, SUB, LANES)
    low = jnp.concatenate([recv[:edge], low_mask])
    high = jnp.concatenate([recv[recv.shape[0] - edge :], high_mask])
    core = lax.axis_index("sites") % 2
    lower_slab = core == 0
    to_chip = [(i, (i + 1 if i % 2 else i - 1) % count) for i in range(count)]
    to_core = [(i, i ^ 1) for i in range(count)]
    across = lax.ppermute(jnp.where(lower_slab, low, high), "sites", to_chip)
    sibling = lax.ppermute(jnp.where(lower_slab, high, low), "sites", to_core)
    core = core.astype(jnp.int32).reshape(1)
    total, edges = inner_moments(recv, present, left)
    total = edge_moments(False, core, sibling, present, left, total, edges)
    total = edge_moments(True, core, across, present, left, total, edges)
    def moved(values, target):
        return lax.ppermute(values, "sites", [(i, target(i)) for i in range(count)])

    for flip in (1, 2, 4):
        total = total + moved(total, lambda i: i ^ flip)
    far, one, other = [moved(total, lambda i: (i + 8 * k) % count) for k in (2, 1, 3)]
    total = (total + far) + (one + other)
    out = jnp.stack([total[:, :n_left], total[:, n_left:]]).reshape(2, MOM, width_group, n_left)
    return jnp.swapaxes(out, 2, 3)[..., None]


def solution(mesh):
    return jax.shard_map(
        per_device,
        mesh=mesh,
        in_specs=(
            P(None, None, None, None, ("cols", "sites"), None),
            P(None, None, "sites", None),
            P("sites", None),
        ),
        out_specs=P(None, None, None, None, "cols"),
        check_vma=False,
    )
```

```python
import functools

import jax
import jax.numpy as jnp
from jax import lax
from jax.experimental import pallas as pl
from jax.experimental.pallas import tpu as pltpu
from jax.sharding import PartitionSpec as P

MOM = 4
HALO = 4
ONSITE_MASS = 0.3
SECOND_HOP = 0.2
BAND_SCALE = 4.5
LANES = 128
SUB = 8
TILES = 4
F32 = jnp.float32


PACK_GROUPS = 4
MERGES = 16


def pack_kernel(in_ref, out_ref, turned):
    columns, groups, slabs, width = in_ref.shape
    lane = lax.broadcasted_iota(jnp.int32, (SUB, LANES), 1)
    odd, high = lane // width % 2 == 1, lane // width >= 2
    swapped = jnp.where(odd, lane - width, lane + width)
    for k in range(groups):
        for base in range(0, slabs, SUB):
            octets = [
                jnp.swapaxes(in_ref[c : c + SUB, k, base : base + SUB, :], 0, 1)
                for c in range(0, columns, SUB)
            ]
            for half in (0, 4):
                rows = [octet[half + s] for s in range(4) for octet in octets]
                turned[(k * slabs + base + half) // 4] = jnp.concatenate(rows, axis=0).T

    @pl.loop(0, groups * slabs // 4 // MERGES)
    def _(i):
        for j in range(MERGES):
            slot = i * MERGES + j
            v = [turned[slot, pl.ds(t, SUB, stride=TILES), :] for t in range(TILES)]
            for p in (0, 2):
                low, upper = v[p], v[p + 1]
                moved = jnp.take_along_axis(jnp.where(odd, low, upper), swapped, axis=1)
                v[p], v[p + 1] = jnp.where(odd, moved, low), jnp.where(odd, upper, moved)
            for p in (0, 1):
                low, upper = v[p], v[p + 2]
                moved = pltpu.roll(jnp.where(high, low, upper), LANES // 2, 1)
                v[p], v[p + 2] = jnp.where(high, moved, low), jnp.where(high, upper, moved)
            for s in range(4):
                out_ref[slot * 4 // slabs, slot * 4 % slabs + s] = v[s]


def pack(pieces):
    columns, groups, slabs, width = pieces.shape
    step = PACK_GROUPS
    out = pl.pallas_call(
        pack_kernel,
        grid=(groups // step,),
        in_specs=[pl.BlockSpec((columns, step, slabs, width), lambda k: (0, k, 0, 0))],
        out_specs=pl.BlockSpec((step, slabs, SUB, LANES), lambda k: (k, 0, 0, 0)),
        out_shape=jax.ShapeDtypeStruct((groups, slabs, SUB, LANES), F32),
        scratch_shapes=[pltpu.VMEM((step * slabs // 4, width, LANES), F32)],
        name="pack",
    )(pieces)
    return out.reshape(groups * slabs, SUB, LANES)


def wrap_masks():
    lane = lax.broadcasted_iota(jnp.int32, (SUB, LANES), 1)
    return lane == 0, lane == LANES - 1


def ahead(tiles, is_last):
    wrapped = jnp.where(is_last, 0.0, pltpu.roll(tiles[0], LANES - 1, 1))
    return tiles[1:] + [wrapped]


def behind(tiles, is_first):
    wrapped = jnp.where(is_first, 0.0, pltpu.roll(tiles[-1], 1, 1))
    return [wrapped] + tiles[:-1]


def stencil_row(level, parity, below, centre, above, old, mask, wraps):
    is_first, is_last = wraps
    T = range(TILES)
    nxt, prv, second = [], [], []
    for r in (0, 1):
        w = centre[r]
        diag = [above[r][t] + below[r][t] for t in T]
        fore, back = ahead(w, is_last), behind(w, is_first)
        if level == 0:
            a = ahead([2.0 * fore[t] - diag[t] for t in T], is_last)
            b = behind([2.0 * back[t] - diag[t] for t in T], is_first)
            second.append([a[t] + b[t] for t in T])
        else:
            a = ahead([fore[t] - diag[t] for t in T], is_last)
            b = behind([back[t] - diag[t] for t in T], is_first)
            second.append([a[t] - b[t] for t in T])
        nxt.append(fore)
        prv.append(back)
    result = []
    for r in (0, 1):
        values = []
        for t in T:
            sign = 1.0 if (parity + t) % 2 == 0 else -1.0
            if level == 0:
                along = prv[1][t] - nxt[1][t] if r == 0 else nxt[0][t] - prv[0][t]
                total = along - (SECOND_HOP * sign) * second[r][t]
            else:
                vertical = above[r][t] if sign > 0 else below[r][t]
                near = (nxt[r][t] + prv[r][t]) + vertical
                turn = -sign if r == 0 else sign
                total = near + (
                    (ONSITE_MASS * sign) * centre[r][t] + (SECOND_HOP * turn) * second[1 - r][t]
                )
            total = total * mask[t]
            values.append(total - old[r][t] if level > 1 else total)
        result.append(values)
    return result


SCALES = (1.0, 1.0 / BAND_SCALE, 2.0 / BAND_SCALE, 2.0 / BAND_SCALE)


def scaled(level, mask):
    return mask if level == 0 else [SCALES[level] * m for m in mask]


def turn_row(src, first):
    return src[pl.ds(first, 16)].reshape(LANES, LANES).T


def product(acc, blocks, left_ref, y):
    for t in range(TILES):
        zero = jnp.zeros((SUB, LANES), F32)
        stacked = [blocks(r, m, h, t) for r in (0, 1) for m in range(MOM) for h in (0, 1)]
        rhs = jnp.concatenate([zero if b is None else b for b in stacked], axis=0)
        term = lax.dot_general(
            rhs.astype(jnp.bfloat16),
            left_ref[y, :, t * LANES : (t + 1) * LANES],
            (((1,), (1,)), ((), ())),
            preferred_element_type=F32,
        )
        acc = term if acc is None else acc + term
    return acc


def inner_kernel(recv_ref, pres_ref, left_ref, sum_ref, edge_ref, field, presb):
    rows = left_ref.shape[0]
    wraps = wrap_masks()
    T = range(TILES)

    @pl.loop(0, rows // 4)
    def _(i):
        for k in range(4):
            y = 4 * i + k
            turned = turn_row(recv_ref, y * 16)
            for t in T:
                mask = jnp.broadcast_to(pres_ref[y, pl.ds(t, 1), :], (SUB, LANES))
                presb[y, t] = mask
                for q in range(4):
                    at = (4 * t + q) * SUB
                    field[0, y, q // 2, q % 2, t] = turned[at : at + SUB] * mask

    def load(level, y, half):
        return [[field[level, y, r, half, t] for t in T] for r in (0, 1)]

    for level in range(MOM):
        first = level + 1

        @pl.loop(0, (rows - 2 * first) // 2)
        def _(i, level=level, first=first):
            y = first + 2 * i
            masks = [scaled(level, [presb[y + k, t] for t in T]) for k in (0, 1)]
            for half in (0, 1):
                window = [load(level, y + k, half) for k in (-1, 0, 1, 2)]
                for k in (0, 1):
                    old = load(level - 1, y + k, half) if level > 1 else None
                    values = stencil_row(
                        level, (first + k) % 2, *window[k : k + 3], old, masks[k], wraps
                    )
                    for r in (0, 1):
                        for t in T:
                            field[(level + 1) % MOM, y + k, r, half, t] = values[r][t]

    for level in range(MOM):
        edge_ref[level, 0] = field[level, level : level + 2]
        edge_ref[level, 1] = field[level, rows - 2 - level : rows - level]
    acc = None
    for y in range(1, rows - 1):

        def blocks(r, m, half, t, y=y):
            return field[(m + 1) % MOM, y, r, half, t] if m < y < rows - 1 - m else None

        acc = product(acc, blocks, left_ref, y)
    sum_ref[...] = acc


def edge_kernel(across, core_ref, src_ref, pres_ref, left_ref, sum_ref, edge_ref, out_ref, field, presb):
    rows = left_ref.shape[0]
    wraps = wrap_masks()
    T = range(TILES)
    tail = HALO * 16

    def side_sum(side):
        base = (-HALO, rows - 2 * HALO)[side]
        for i in range(HALO):
            j = i if side == 0 else 2 * HALO + i
            turned = turn_row(src_ref, i * 16)
            for t in T:
                at = i * TILES + t
                row = src_ref[tail + at // SUB, pl.ds(at % SUB, 1), :]
                mask = jnp.broadcast_to(row, (SUB, LANES))
                presb[j, t] = mask
                for q in range(4):
                    at = (4 * t + q) * SUB
                    field[0, j, q // 2, q % 2, t] = turned[at : at + SUB] * mask
        for j in range(HALO, 2 * HALO):
            for t in T:
                presb[j, t] = jnp.broadcast_to(pres_ref[base + j, pl.ds(t, 1), :], (SUB, LANES))

        def tile(level, j, r, half, t):
            first = HALO + level if side == 0 else 2 * HALO - 2 - level
            if first <= j < first + 2:
                return edge_ref[level, side, j - first, r, half, t]
            return field[level, j, r, half, t]

        def load(level, j, half):
            return [[tile(level, j, r, half, t) for t in T] for r in (0, 1)]

        for level in range(MOM):
            first = 1 + level if side == 0 else 2 * HALO - 1 - level
            for half in (0, 1):
                window = [load(level, first + k, half) for k in range(-1, 5)]
                for k in range(4):
                    j = first + k
                    mask = scaled(level, [presb[j, t] for t in T])
                    old = load(level - 1, j, half) if level > 1 else None
                    values = stencil_row(level, j % 2, *window[k : k + 3], old, mask, wraps)
                    for r in (0, 1):
                        for t in T:
                            field[(level + 1) % MOM, j, r, half, t] = values[r][t]

        acc = sum_ref[...]
        for y in range(HALO) if side == 0 else range(rows - HALO, rows):

            def blocks(r, m, half, t, y=y):
                if m < y < rows - 1 - m:
                    return None
                return field[(m + 1) % MOM, y - base, r, half, t]

            acc = product(acc, blocks, left_ref, y)
        if across:
            half_rows = MOM * 2 * SUB
            top, bottom = acc[:half_rows], acc[half_rows:]
            lane_out = lax.broadcasted_iota(jnp.int32, top.shape, 1)
            acc = pltpu.roll(bottom, LANES // 2, 1) + jnp.where(lane_out < LANES // 2, top, -top)
        out_ref[...] = acc

    for core in (0, 1):

        @pl.when(core_ref[0] == core)
        def _(side=core if across else 1 - core):
            side_sum(side)


ROW = (2, 2, TILES, SUB, LANES)


def inner_moments(recv, pres, left):
    rows, n2, _ = left.shape
    vm = pl.BlockSpec(memory_space=pltpu.VMEM)
    return pl.pallas_call(
        inner_kernel,
        in_specs=[vm] * 3,
        out_specs=[vm] * 2,
        out_shape=[
            jax.ShapeDtypeStruct((2 * MOM * 2 * SUB, n2), F32),
            jax.ShapeDtypeStruct((MOM, 2, 2, *ROW), F32),
        ],
        scratch_shapes=[
            pltpu.VMEM((MOM, rows, *ROW), F32),
            pltpu.VMEM((rows, TILES, SUB, LANES), F32),
        ],
        compiler_params=pltpu.CompilerParams(vmem_limit_bytes=40 * 2**20),
        cost_estimate=pl.CostEstimate(flops=10**9, bytes_accessed=10**7, transcendentals=0),
        name="inner_moments",
    )(recv, pres, left)


def edge_moments(across, core, src, pres, left, total, edges):
    n2 = left.shape[1]
    vm = pl.BlockSpec(memory_space=pltpu.VMEM)
    return pl.pallas_call(
        functools.partial(edge_kernel, across),
        in_specs=[pl.BlockSpec(memory_space=pltpu.SMEM)] + [vm] * 5,
        out_specs=vm,
        out_shape=jax.ShapeDtypeStruct(((1 if across else 2) * MOM * 2 * SUB, n2), F32),
        scratch_shapes=[
            pltpu.VMEM((MOM, 3 * HALO, *ROW), F32),
            pltpu.VMEM((3 * HALO, TILES, SUB, LANES), F32),
        ],
        compiler_params=pltpu.CompilerParams(vmem_limit_bytes=40 * 2**20),
        cost_estimate=pl.CostEstimate(flops=10**8, bytes_accessed=10**6, transcendentals=0),
        name="edge_across" if across else "edge_sibling",
    )(core, src, pres, left, total, edges)


def last_sum_kernel(mine_ref, far_ref, one_ref, other_ref, out_ref):
    total = (mine_ref[...] + far_ref[...]) + (one_ref[...] + other_ref[...])
    half = out_ref.shape[2]
    out_ref[0] = total[:, :half]
    out_ref[1] = total[:, half:]


def last_sum(mine, far, one, other):
    rows, width = mine.shape
    vm = pl.BlockSpec(memory_space=pltpu.VMEM)
    return pl.pallas_call(
        last_sum_kernel,
        in_specs=[vm] * 4,
        out_specs=vm,
        out_shape=jax.ShapeDtypeStruct((2, rows, width // 2), F32),
        compiler_params=pltpu.CompilerParams(vmem_limit_bytes=8 * 2**20),
        name="last_sum",
    )(mine, far, one, other)


def per_device(right_vectors, left_vectors, vacancy):
    parts, width_group, groups, slabs, _, piece = right_vectors.shape
    count = lax.axis_size("sites")
    n_left, rows, width = left_vectors.shape[1:]

    packed = pack(right_vectors.reshape(parts * width_group, groups, slabs, piece))
    packed, left_vectors = lax.optimization_barrier((packed, left_vectors))
    recv = lax.all_to_all(packed, ("cols", "sites"), 0, 0, tiled=True)

    site = lax.broadcasted_iota(jnp.int32, (width, width), 0)
    place = lax.broadcasted_iota(jnp.int32, (width, width), 1)
    to_place = (site % TILES * LANES + site // TILES == place).astype(jnp.bfloat16)
    left = left_vectors.reshape(2 * n_left * rows, width)
    left = jnp.dot(left, to_place, preferred_element_type=jnp.bfloat16)
    left = jnp.swapaxes(left.reshape(2 * n_left, rows, width), 0, 1)
    present = jnp.dot(vacancy.astype(jnp.bfloat16), to_place, preferred_element_type=F32)
    present = present.reshape(rows, TILES, LANES)
    recv, left, present = lax.optimization_barrier((recv, left, present))

    edge = HALO * width // piece
    low_mask = present[:HALO].reshape(-1, SUB, LANES)
    high_mask = present[rows - HALO :].reshape(-1, SUB, LANES)
    low = jnp.concatenate([recv[:edge], low_mask])
    high = jnp.concatenate([recv[recv.shape[0] - edge :], high_mask])
    core = lax.axis_index("sites") % 2
    lower_slab = core == 0
    to_chip = [(i, (i + 1 if i % 2 else i - 1) % count) for i in range(count)]
    to_core = [(i, i ^ 1) for i in range(count)]
    across = lax.ppermute(jnp.where(lower_slab, low, high), "sites", to_chip)
    sibling = lax.ppermute(jnp.where(lower_slab, high, low), "sites", to_core)
    core = core.astype(jnp.int32).reshape(1)
    total, edges = inner_moments(recv, present, left)
    total = edge_moments(False, core, sibling, present, left, total, edges)
    total = edge_moments(True, core, across, present, left, total, edges)
    def moved(values, target):
        return lax.ppermute(values, "sites", [(i, target(i)) for i in range(count)])

    for flip in (1, 2, 4):
        total = total + moved(total, lambda i: i ^ flip)
    far, one, other = [moved(total, lambda i: (i + 8 * k) % count) for k in (2, 1, 3)]
    out = last_sum(total, far, one, other).reshape(2, MOM, width_group, n_left)
    return jnp.swapaxes(out, 2, 3)[..., None]


def solution(mesh):
    return jax.shard_map(
        per_device,
        mesh=mesh,
        in_specs=(
            P(None, None, None, None, ("cols", "sites"), None),
            P(None, None, "sites", None),
            P("sites", None),
        ),
        out_specs=P(None, None, None, None, "cols"),
        check_vma=False,
    )
```

```python
import functools

import jax
import jax.numpy as jnp
from jax import lax
from jax.experimental import pallas as pl
from jax.experimental.pallas import tpu as pltpu
from jax.sharding import PartitionSpec as P

MOM = 4
HALO = 4
ONSITE_MASS = 0.3
SECOND_HOP = 0.2
BAND_SCALE = 4.5
LANES = 128
SUB = 8
TILES = 4
F32 = jnp.float32


PACK_GROUPS = 4
MERGES = 16


def pack_kernel(in_ref, out_ref, turned):
    columns, groups, slabs, width = in_ref.shape
    lane = lax.broadcasted_iota(jnp.int32, (SUB, LANES), 1)
    odd, high = lane // width % 2 == 1, lane // width >= 2
    swapped = jnp.where(odd, lane - width, lane + width)
    for k in range(groups):
        for base in range(0, slabs, SUB):
            octets = [
                jnp.swapaxes(in_ref[c : c + SUB, k, base : base + SUB, :], 0, 1)
                for c in range(0, columns, SUB)
            ]
            for half in (0, 4):
                rows = [octet[half + s] for s in range(4) for octet in octets]
                turned[(k * slabs + base + half) // 4] = jnp.concatenate(rows, axis=0).T

    @pl.loop(0, groups * slabs // 4 // MERGES)
    def _(i):
        for j in range(MERGES):
            slot = i * MERGES + j
            v = [turned[slot, pl.ds(t, SUB, stride=TILES), :] for t in range(TILES)]
            for p in (0, 2):
                low, upper = v[p], v[p + 1]
                moved = jnp.take_along_axis(jnp.where(odd, low, upper), swapped, axis=1)
                v[p], v[p + 1] = jnp.where(odd, moved, low), jnp.where(odd, upper, moved)
            for p in (0, 1):
                low, upper = v[p], v[p + 2]
                moved = pltpu.roll(jnp.where(high, low, upper), LANES // 2, 1)
                v[p], v[p + 2] = jnp.where(high, moved, low), jnp.where(high, upper, moved)
            for s in range(4):
                out_ref[slot * 4 // slabs, slot * 4 % slabs + s] = v[s]


def pack(pieces):
    columns, groups, slabs, width = pieces.shape
    step = PACK_GROUPS
    out = pl.pallas_call(
        pack_kernel,
        grid=(groups // step,),
        in_specs=[pl.BlockSpec((columns, step, slabs, width), lambda k: (0, k, 0, 0))],
        out_specs=pl.BlockSpec((step, slabs, SUB, LANES), lambda k: (k, 0, 0, 0)),
        out_shape=jax.ShapeDtypeStruct((groups, slabs, SUB, LANES), F32),
        scratch_shapes=[pltpu.VMEM((step * slabs // 4, width, LANES), F32)],
        name="pack",
    )(pieces)
    return out.reshape(groups * slabs, SUB, LANES)


def wrap_masks():
    lane = lax.broadcasted_iota(jnp.int32, (SUB, LANES), 1)
    return lane == 0, lane == LANES - 1


def ahead(tiles, is_last):
    wrapped = jnp.where(is_last, 0.0, pltpu.roll(tiles[0], LANES - 1, 1))
    return tiles[1:] + [wrapped]


def behind(tiles, is_first):
    wrapped = jnp.where(is_first, 0.0, pltpu.roll(tiles[-1], 1, 1))
    return [wrapped] + tiles[:-1]


def stencil_row(level, parity, below, centre, above, old, mask, wraps):
    is_first, is_last = wraps
    T = range(TILES)
    nxt, prv, second = [], [], []
    for r in (0, 1):
        w = centre[r]
        diag = [above[r][t] + below[r][t] for t in T]
        fore, back = ahead(w, is_last), behind(w, is_first)
        if level == 0:
            a = ahead([2.0 * fore[t] - diag[t] for t in T], is_last)
            b = behind([2.0 * back[t] - diag[t] for t in T], is_first)
            second.append([a[t] + b[t] for t in T])
        else:
            a = ahead([fore[t] - diag[t] for t in T], is_last)
            b = behind([back[t] - diag[t] for t in T], is_first)
            second.append([a[t] - b[t] for t in T])
        nxt.append(fore)
        prv.append(back)
    result = []
    for r in (0, 1):
        values = []
        for t in T:
            sign = 1.0 if (parity + t) % 2 == 0 else -1.0
            if level == 0:
                along = prv[1][t] - nxt[1][t] if r == 0 else nxt[0][t] - prv[0][t]
                total = along - (SECOND_HOP * sign) * second[r][t]
            else:
                vertical = above[r][t] if sign > 0 else below[r][t]
                near = (nxt[r][t] + prv[r][t]) + vertical
                turn = -sign if r == 0 else sign
                total = near + (
                    (ONSITE_MASS * sign) * centre[r][t] + (SECOND_HOP * turn) * second[1 - r][t]
                )
            total = total * mask[t]
            values.append(total - old[r][t] if level > 1 else total)
        result.append(values)
    return result


SCALES = (1.0, 1.0 / BAND_SCALE, 2.0 / BAND_SCALE, 2.0 / BAND_SCALE)


def scaled(level, mask):
    return mask if level == 0 else [SCALES[level] * m for m in mask]


def turn_row(src, first):
    return src[pl.ds(first, 16)].reshape(LANES, LANES).T


def product(acc, blocks, left_ref, y):
    for t in range(TILES):
        zero = jnp.zeros((SUB, LANES), F32)
        stacked = [blocks(r, m, h, t) for r in (0, 1) for m in range(MOM) for h in (0, 1)]
        rhs = jnp.concatenate([zero if b is None else b for b in stacked], axis=0)
        term = lax.dot_general(
            rhs.astype(jnp.bfloat16),
            left_ref[y, :, t * LANES : (t + 1) * LANES],
            (((1,), (1,)), ((), ())),
            preferred_element_type=F32,
        )
        acc = term if acc is None else acc + term
    return acc


def inner_kernel(recv_ref, pres_ref, left_ref, sum_ref, edge_ref, field, presb):
    rows = left_ref.shape[0]
    wraps = wrap_masks()
    T = range(TILES)

    @pl.loop(0, rows // 4)
    def _(i):
        for k in range(4):
            y = 4 * i + k
            turned = turn_row(recv_ref, y * 16)
            for t in T:
                mask = jnp.broadcast_to(pres_ref[y, pl.ds(t, 1), :], (SUB, LANES))
                presb[y, t] = mask
                for q in range(4):
                    at = (4 * t + q) * SUB
                    field[0, y, q // 2, q % 2, t] = turned[at : at + SUB] * mask

    def load(level, y, half):
        return [[field[level, y, r, half, t] for t in T] for r in (0, 1)]

    for level in range(MOM):
        first = level + 1

        @pl.loop(0, (rows - 2 * first) // 2)
        def _(i, level=level, first=first):
            y = first + 2 * i
            masks = [scaled(level, [presb[y + k, t] for t in T]) for k in (0, 1)]
            for half in (0, 1):
                window = [load(level, y + k, half) for k in (-1, 0, 1, 2)]
                for k in (0, 1):
                    old = load(level - 1, y + k, half) if level > 1 else None
                    values = stencil_row(
                        level, (first + k) % 2, *window[k : k + 3], old, masks[k], wraps
                    )
                    for r in (0, 1):
                        for t in T:
                            field[(level + 1) % MOM, y + k, r, half, t] = values[r][t]

    for level in range(MOM):
        edge_ref[level, 0] = field[level, level : level + 2]
        edge_ref[level, 1] = field[level, rows - 2 - level : rows - level]
    acc = None
    for y in range(1, rows - 1):

        def blocks(r, m, half, t, y=y):
            return field[(m + 1) % MOM, y, r, half, t] if m < y < rows - 1 - m else None

        acc = product(acc, blocks, left_ref, y)
    sum_ref[...] = acc


def edge_kernel(across, core_ref, src_ref, pres_ref, left_ref, sum_ref, edge_ref, out_ref, field, presb):
    rows = left_ref.shape[0]
    wraps = wrap_masks()
    T = range(TILES)
    tail = HALO * 16

    def side_sum(side):
        base = (-HALO, rows - 2 * HALO)[side]
        for i in range(HALO):
            j = i if side == 0 else 2 * HALO + i
            turned = turn_row(src_ref, i * 16)
            for t in T:
                at = i * TILES + t
                row = src_ref[tail + at // SUB, pl.ds(at % SUB, 1), :]
                mask = jnp.broadcast_to(row, (SUB, LANES))
                presb[j, t] = mask
                for q in range(4):
                    at = (4 * t + q) * SUB
                    field[0, j, q // 2, q % 2, t] = turned[at : at + SUB] * mask
        for j in range(HALO, 2 * HALO):
            for t in T:
                presb[j, t] = jnp.broadcast_to(pres_ref[base + j, pl.ds(t, 1), :], (SUB, LANES))

        def tile(level, j, r, half, t):
            first = HALO + level if side == 0 else 2 * HALO - 2 - level
            if first <= j < first + 2:
                return edge_ref[level, side, j - first, r, half, t]
            return field[level, j, r, half, t]

        def load(level, j, half):
            return [[tile(level, j, r, half, t) for t in T] for r in (0, 1)]

        for level in range(MOM):
            first = 1 + level if side == 0 else 2 * HALO - 1 - level
            for half in (0, 1):
                window = [load(level, first + k, half) for k in range(-1, 5)]
                for k in range(4):
                    j = first + k
                    mask = scaled(level, [presb[j, t] for t in T])
                    old = load(level - 1, j, half) if level > 1 else None
                    values = stencil_row(level, j % 2, *window[k : k + 3], old, mask, wraps)
                    for r in (0, 1):
                        for t in T:
                            field[(level + 1) % MOM, j, r, half, t] = values[r][t]

        acc = sum_ref[...]
        for y in range(HALO) if side == 0 else range(rows - HALO, rows):

            def blocks(r, m, half, t, y=y):
                if m < y < rows - 1 - m:
                    return None
                return field[(m + 1) % MOM, y - base, r, half, t]

            acc = product(acc, blocks, left_ref, y)
        if across:
            half_rows = MOM * 2 * SUB
            top, bottom = acc[:half_rows], acc[half_rows:]
            lane_out = lax.broadcasted_iota(jnp.int32, top.shape, 1)
            acc = pltpu.roll(bottom, LANES // 2, 1) + jnp.where(lane_out < LANES // 2, top, -top)
        out_ref[...] = acc

    for core in (0, 1):

        @pl.when(core_ref[0] == core)
        def _(side=core if across else 1 - core):
            side_sum(side)


ROW = (2, 2, TILES, SUB, LANES)


def inner_moments(recv, pres, left):
    rows, n2, _ = left.shape
    vm = pl.BlockSpec(memory_space=pltpu.VMEM)
    return pl.pallas_call(
        inner_kernel,
        in_specs=[vm] * 3,
        out_specs=[vm] * 2,
        out_shape=[
            jax.ShapeDtypeStruct((2 * MOM * 2 * SUB, n2), F32),
            jax.ShapeDtypeStruct((MOM, 2, 2, *ROW), F32),
        ],
        scratch_shapes=[
            pltpu.VMEM((MOM, rows, *ROW), F32),
            pltpu.VMEM((rows, TILES, SUB, LANES), F32),
        ],
        compiler_params=pltpu.CompilerParams(vmem_limit_bytes=40 * 2**20),
        cost_estimate=pl.CostEstimate(flops=10**9, bytes_accessed=10**7, transcendentals=0),
        name="inner_moments",
    )(recv, pres, left)


def edge_moments(across, core, src, pres, left, total, edges):
    n2 = left.shape[1]
    vm = pl.BlockSpec(memory_space=pltpu.VMEM)
    return pl.pallas_call(
        functools.partial(edge_kernel, across),
        in_specs=[pl.BlockSpec(memory_space=pltpu.SMEM)] + [vm] * 5,
        out_specs=vm,
        out_shape=jax.ShapeDtypeStruct(((1 if across else 2) * MOM * 2 * SUB, n2), F32),
        scratch_shapes=[
            pltpu.VMEM((MOM, 3 * HALO, *ROW), F32),
            pltpu.VMEM((3 * HALO, TILES, SUB, LANES), F32),
        ],
        compiler_params=pltpu.CompilerParams(vmem_limit_bytes=40 * 2**20),
        cost_estimate=pl.CostEstimate(flops=10**8, bytes_accessed=10**6, transcendentals=0),
        name="edge_across" if across else "edge_sibling",
    )(core, src, pres, left, total, edges)


def last_sum_kernel(mine_ref, far_ref, one_ref, other_ref, out_ref):
    total = (mine_ref[...] + far_ref[...]) + (one_ref[...] + other_ref[...])
    half = out_ref.shape[2]
    out_ref[0] = total[:, :half]
    out_ref[1] = total[:, half:]


def last_sum(mine, far, one, other):
    rows, width = mine.shape
    vm = pl.BlockSpec(memory_space=pltpu.VMEM)
    return pl.pallas_call(
        last_sum_kernel,
        in_specs=[vm] * 4,
        out_specs=vm,
        out_shape=jax.ShapeDtypeStruct((2, rows, width // 2), F32),
        compiler_params=pltpu.CompilerParams(vmem_limit_bytes=8 * 2**20),
        name="last_sum",
    )(mine, far, one, other)


def per_device(right_vectors, left_vectors, vacancy):
    parts, width_group, groups, slabs, _, piece = right_vectors.shape
    count = lax.axis_size("sites")
    n_left, rows, width = left_vectors.shape[1:]

    packed = pack(right_vectors.reshape(parts * width_group, groups, slabs, piece))
    packed, left_vectors = lax.optimization_barrier((packed, left_vectors))
    recv = lax.all_to_all(packed, ("cols", "sites"), 0, 0, tiled=True)

    site = lax.broadcasted_iota(jnp.int32, (width, width), 0)
    place = lax.broadcasted_iota(jnp.int32, (width, width), 1)
    to_place = (site % TILES * LANES + site // TILES == place).astype(jnp.bfloat16)
    left = left_vectors.reshape(2 * n_left * rows, width)
    left = jnp.dot(left, to_place, preferred_element_type=jnp.bfloat16)
    left = jnp.swapaxes(left.reshape(2 * n_left, rows, width), 0, 1)
    present = jnp.dot(vacancy.astype(jnp.bfloat16), to_place, preferred_element_type=F32)
    present = present.reshape(rows, TILES, LANES)
    recv, left, present = lax.optimization_barrier((recv, left, present))

    edge = HALO * width // piece
    low_mask = present[:HALO].reshape(-1, SUB, LANES)
    high_mask = present[rows - HALO :].reshape(-1, SUB, LANES)
    low = jnp.concatenate([recv[:edge], low_mask])
    high = jnp.concatenate([recv[recv.shape[0] - edge :], high_mask])
    core = lax.axis_index("sites") % 2
    lower_slab = core == 0
    to_chip = [(i, (i + 1 if i % 2 else i - 1) % count) for i in range(count)]
    to_core = [(i, i ^ 1) for i in range(count)]
    across = lax.ppermute(jnp.where(lower_slab, low, high), "sites", to_chip)
    sibling = lax.ppermute(jnp.where(lower_slab, high, low), "sites", to_core)
    core = core.astype(jnp.int32).reshape(1)
    total, edges = inner_moments(recv, present, left)
    total = edge_moments(False, core, sibling, present, left, total, edges)
    total = edge_moments(True, core, across, present, left, total, edges)
    def moved(values, flip):
        return lax.ppermute(values, "sites", [(i, i ^ flip) for i in range(count)])

    total = total + moved(total, 1)
    z_near, y_near, both = moved(total, 2), moved(total, 8), moved(total, 10)
    total = (total + z_near) + (y_near + both)
    z_far, y_far, both = moved(total, 4), moved(total, 24), moved(total, 28)
    out = last_sum(total, z_far, y_far, both).reshape(2, MOM, width_group, n_left)
    return jnp.swapaxes(out, 2, 3)[..., None]


def solution(mesh):
    return jax.shard_map(
        per_device,
        mesh=mesh,
        in_specs=(
            P(None, None, None, None, ("cols", "sites"), None),
            P(None, None, "sites", None),
            P("sites", None),
        ),
        out_specs=P(None, None, None, None, "cols"),
        check_vma=False,
    )
```

```python
import functools

import jax
import jax.numpy as jnp
from jax import lax
from jax.experimental import pallas as pl
from jax.experimental.pallas import tpu as pltpu
from jax.sharding import PartitionSpec as P

MOM = 4
HALO = 4
ONSITE_MASS = 0.3
SECOND_HOP = 0.2
BAND_SCALE = 4.5
LANES = 128
SUB = 8
TILES = 4
F32 = jnp.float32


PACK_GROUPS = 4
MERGES = 16


def pack_kernel(in_ref, out_ref, turned):
    columns, groups, slabs, width = in_ref.shape
    lane = lax.broadcasted_iota(jnp.int32, (SUB, LANES), 1)
    odd, high = lane // width % 2 == 1, lane // width >= 2
    swapped = jnp.where(odd, lane - width, lane + width)
    for k in range(groups):
        for base in range(0, slabs, SUB):
            octets = [
                jnp.swapaxes(in_ref[c : c + SUB, k, base : base + SUB, :], 0, 1)
                for c in range(0, columns, SUB)
            ]
            for half in (0, 4):
                rows = [octet[half + s] for s in range(4) for octet in octets]
                turned[(k * slabs + base + half) // 4] = jnp.concatenate(rows, axis=0).T

    @pl.loop(0, groups * slabs // 4 // MERGES)
    def _(i):
        for j in range(MERGES):
            slot = i * MERGES + j
            v = [turned[slot, pl.ds(t, SUB, stride=TILES), :] for t in range(TILES)]
            for p in (0, 2):
                low, upper = v[p], v[p + 1]
                moved = jnp.take_along_axis(jnp.where(odd, low, upper), swapped, axis=1)
                v[p], v[p + 1] = jnp.where(odd, moved, low), jnp.where(odd, upper, moved)
            for p in (0, 1):
                low, upper = v[p], v[p + 2]
                moved = pltpu.roll(jnp.where(high, low, upper), LANES // 2, 1)
                v[p], v[p + 2] = jnp.where(high, moved, low), jnp.where(high, upper, moved)
            for s in range(4):
                out_ref[slot * 4 // slabs, slot * 4 % slabs + s] = v[s]


def pack(pieces):
    columns, groups, slabs, width = pieces.shape
    step = PACK_GROUPS
    out = pl.pallas_call(
        pack_kernel,
        grid=(groups // step,),
        in_specs=[pl.BlockSpec((columns, step, slabs, width), lambda k: (0, k, 0, 0))],
        out_specs=pl.BlockSpec((step, slabs, SUB, LANES), lambda k: (k, 0, 0, 0)),
        out_shape=jax.ShapeDtypeStruct((groups, slabs, SUB, LANES), F32),
        scratch_shapes=[pltpu.VMEM((step * slabs // 4, width, LANES), F32)],
        name="pack",
    )(pieces)
    return out.reshape(groups * slabs, SUB, LANES)


def wrap_masks():
    lane = lax.broadcasted_iota(jnp.int32, (SUB, LANES), 1)
    return lane == 0, lane == LANES - 1


def ahead(tiles, is_last):
    wrapped = jnp.where(is_last, 0.0, pltpu.roll(tiles[0], LANES - 1, 1))
    return tiles[1:] + [wrapped]


def behind(tiles, is_first):
    wrapped = jnp.where(is_first, 0.0, pltpu.roll(tiles[-1], 1, 1))
    return [wrapped] + tiles[:-1]


def stencil_row(level, parity, below, centre, above, old, mask, wraps):
    is_first, is_last = wraps
    T = range(TILES)
    nxt, prv, second = [], [], []
    for r in (0, 1):
        w = centre[r]
        diag = [above[r][t] + below[r][t] for t in T]
        fore, back = ahead(w, is_last), behind(w, is_first)
        if level == 0:
            a = ahead([2.0 * fore[t] - diag[t] for t in T], is_last)
            b = behind([2.0 * back[t] - diag[t] for t in T], is_first)
            second.append([a[t] + b[t] for t in T])
        else:
            a = ahead([fore[t] - diag[t] for t in T], is_last)
            b = behind([back[t] - diag[t] for t in T], is_first)
            second.append([a[t] - b[t] for t in T])
        nxt.append(fore)
        prv.append(back)
    result = []
    for r in (0, 1):
        values = []
        for t in T:
            sign = 1.0 if (parity + t) % 2 == 0 else -1.0
            if level == 0:
                along = prv[1][t] - nxt[1][t] if r == 0 else nxt[0][t] - prv[0][t]
                total = along - (SECOND_HOP * sign) * second[r][t]
            else:
                vertical = above[r][t] if sign > 0 else below[r][t]
                near = (nxt[r][t] + prv[r][t]) + vertical
                turn = -sign if r == 0 else sign
                total = near + (
                    (ONSITE_MASS * sign) * centre[r][t] + (SECOND_HOP * turn) * second[1 - r][t]
                )
            total = total * mask[t]
            values.append(total - old[r][t] if level > 1 else total)
        result.append(values)
    return result


SCALES = (1.0, 1.0 / BAND_SCALE, 2.0 / BAND_SCALE, 2.0 / BAND_SCALE)


def scaled(level, mask):
    return mask if level == 0 else [SCALES[level] * m for m in mask]


def turn_row(src, first):
    return src[pl.ds(first, 16)].reshape(LANES, LANES).T


def product(acc, blocks, left_ref, y):
    for t in range(TILES):
        zero = jnp.zeros((SUB, LANES), F32)
        stacked = [blocks(r, m, h, t) for r in (0, 1) for m in range(MOM) for h in (0, 1)]
        rhs = jnp.concatenate([zero if b is None else b for b in stacked], axis=0)
        term = lax.dot_general(
            rhs.astype(jnp.bfloat16),
            left_ref[y, :, t * LANES : (t + 1) * LANES],
            (((1,), (1,)), ((), ())),
            preferred_element_type=F32,
        )
        acc = term if acc is None else acc + term
    return acc


def inner_kernel(recv_ref, pres_ref, left_ref, sum_ref, edge_ref, field, presb):
    rows = left_ref.shape[0]
    wraps = wrap_masks()
    T = range(TILES)

    @pl.loop(0, rows // 4)
    def _(i):
        for k in range(4):
            y = 4 * i + k
            turned = turn_row(recv_ref, y * 16)
            for t in T:
                mask = jnp.broadcast_to(pres_ref[y, pl.ds(t, 1), :], (SUB, LANES))
                presb[y, t] = mask
                for q in range(4):
                    at = (4 * t + q) * SUB
                    field[0, y, q // 2, q % 2, t] = turned[at : at + SUB] * mask

    def load(level, y, half):
        return [[field[level, y, r, half, t] for t in T] for r in (0, 1)]

    for level in range(MOM):
        first = level + 1

        @pl.loop(0, (rows - 2 * first) // 2)
        def _(i, level=level, first=first):
            y = first + 2 * i
            masks = [scaled(level, [presb[y + k, t] for t in T]) for k in (0, 1)]
            for half in (0, 1):
                window = [load(level, y + k, half) for k in (-1, 0, 1, 2)]
                for k in (0, 1):
                    old = load(level - 1, y + k, half) if level > 1 else None
                    values = stencil_row(
                        level, (first + k) % 2, *window[k : k + 3], old, masks[k], wraps
                    )
                    for r in (0, 1):
                        for t in T:
                            field[(level + 1) % MOM, y + k, r, half, t] = values[r][t]

    for level in range(MOM):
        edge_ref[level, 0] = field[level, level : level + 2]
        edge_ref[level, 1] = field[level, rows - 2 - level : rows - level]
    acc = None
    for y in range(1, rows - 1):

        def blocks(r, m, half, t, y=y):
            return field[(m + 1) % MOM, y, r, half, t] if m < y < rows - 1 - m else None

        acc = product(acc, blocks, left_ref, y)
    sum_ref[...] = acc


def edge_kernel(across, core_ref, src_ref, pres_ref, left_ref, sum_ref, edge_ref, out_ref, field, presb):
    rows = left_ref.shape[0]
    wraps = wrap_masks()
    T = range(TILES)
    tail = HALO * 16

    def side_sum(side):
        base = (-HALO, rows - 2 * HALO)[side]
        for i in range(HALO):
            j = i if side == 0 else 2 * HALO + i
            turned = turn_row(src_ref, i * 16)
            for t in T:
                at = i * TILES + t
                row = src_ref[tail + at // SUB, pl.ds(at % SUB, 1), :]
                mask = jnp.broadcast_to(row, (SUB, LANES))
                presb[j, t] = mask
                for q in range(4):
                    at = (4 * t + q) * SUB
                    field[0, j, q // 2, q % 2, t] = turned[at : at + SUB] * mask
        for j in range(HALO, 2 * HALO):
            for t in T:
                presb[j, t] = jnp.broadcast_to(pres_ref[base + j, pl.ds(t, 1), :], (SUB, LANES))

        def tile(level, j, r, half, t):
            first = HALO + level if side == 0 else 2 * HALO - 2 - level
            if first <= j < first + 2:
                return edge_ref[level, side, j - first, r, half, t]
            return field[level, j, r, half, t]

        def load(level, j, half):
            return [[tile(level, j, r, half, t) for t in T] for r in (0, 1)]

        for level in range(MOM):
            first = 1 + level if side == 0 else 2 * HALO - 1 - level
            for half in (0, 1):
                window = [load(level, first + k, half) for k in range(-1, 5)]
                for k in range(4):
                    j = first + k
                    mask = scaled(level, [presb[j, t] for t in T])
                    old = load(level - 1, j, half) if level > 1 else None
                    values = stencil_row(level, j % 2, *window[k : k + 3], old, mask, wraps)
                    for r in (0, 1):
                        for t in T:
                            field[(level + 1) % MOM, j, r, half, t] = values[r][t]

        acc = sum_ref[...]
        for y in range(HALO) if side == 0 else range(rows - HALO, rows):

            def blocks(r, m, half, t, y=y):
                if m < y < rows - 1 - m:
                    return None
                return field[(m + 1) % MOM, y - base, r, half, t]

            acc = product(acc, blocks, left_ref, y)
        if across:
            half_rows = MOM * 2 * SUB
            top, bottom = acc[:half_rows], acc[half_rows:]
            lane_out = lax.broadcasted_iota(jnp.int32, top.shape, 1)
            acc = pltpu.roll(bottom, LANES // 2, 1) + jnp.where(lane_out < LANES // 2, top, -top)
        out_ref[...] = acc

    for core in (0, 1):

        @pl.when(core_ref[0] == core)
        def _(side=core if across else 1 - core):
            side_sum(side)


ROW = (2, 2, TILES, SUB, LANES)


def inner_moments(recv, pres, left):
    rows, n2, _ = left.shape
    vm = pl.BlockSpec(memory_space=pltpu.VMEM)
    return pl.pallas_call(
        inner_kernel,
        in_specs=[vm] * 3,
        out_specs=[vm] * 2,
        out_shape=[
            jax.ShapeDtypeStruct((2 * MOM * 2 * SUB, n2), F32),
            jax.ShapeDtypeStruct((MOM, 2, 2, *ROW), F32),
        ],
        scratch_shapes=[
            pltpu.VMEM((MOM, rows, *ROW), F32),
            pltpu.VMEM((rows, TILES, SUB, LANES), F32),
        ],
        compiler_params=pltpu.CompilerParams(vmem_limit_bytes=40 * 2**20),
        cost_estimate=pl.CostEstimate(flops=10**9, bytes_accessed=10**7, transcendentals=0),
        name="inner_moments",
    )(recv, pres, left)


def edge_moments(across, core, src, pres, left, total, edges):
    n2 = left.shape[1]
    vm = pl.BlockSpec(memory_space=pltpu.VMEM)
    return pl.pallas_call(
        functools.partial(edge_kernel, across),
        in_specs=[pl.BlockSpec(memory_space=pltpu.SMEM)] + [vm] * 5,
        out_specs=vm,
        out_shape=jax.ShapeDtypeStruct(((1 if across else 2) * MOM * 2 * SUB, n2), F32),
        scratch_shapes=[
            pltpu.VMEM((MOM, 3 * HALO, *ROW), F32),
            pltpu.VMEM((3 * HALO, TILES, SUB, LANES), F32),
        ],
        compiler_params=pltpu.CompilerParams(vmem_limit_bytes=40 * 2**20),
        cost_estimate=pl.CostEstimate(flops=10**8, bytes_accessed=10**6, transcendentals=0),
        name="edge_across" if across else "edge_sibling",
    )(core, src, pres, left, total, edges)


def last_sum_kernel(mine_ref, far_ref, one_ref, other_ref, out_ref):
    total = (mine_ref[...] + far_ref[...]) + (one_ref[...] + other_ref[...])
    half = out_ref.shape[2]
    out_ref[0] = total[:, :half]
    out_ref[1] = total[:, half:]


def last_sum(mine, far, one, other):
    rows, width = mine.shape
    vm = pl.BlockSpec(memory_space=pltpu.VMEM)
    return pl.pallas_call(
        last_sum_kernel,
        in_specs=[vm] * 4,
        out_specs=vm,
        out_shape=jax.ShapeDtypeStruct((2, rows, width // 2), F32),
        compiler_params=pltpu.CompilerParams(vmem_limit_bytes=8 * 2**20),
        name="last_sum",
    )(mine, far, one, other)


def per_device(right_vectors, left_vectors, vacancy):
    parts, width_group, groups, slabs, _, piece = right_vectors.shape
    count = lax.axis_size("sites")
    n_left, rows, width = left_vectors.shape[1:]

    packed = pack(right_vectors.reshape(parts * width_group, groups, slabs, piece))
    packed, left_vectors = lax.optimization_barrier((packed, left_vectors))
    recv = lax.all_to_all(packed, ("cols", "sites"), 0, 0, tiled=True)

    site = lax.broadcasted_iota(jnp.int32, (width, width), 0)
    place = lax.broadcasted_iota(jnp.int32, (width, width), 1)
    to_place = (site % TILES * LANES + site // TILES == place).astype(jnp.bfloat16)
    left = left_vectors.reshape(2 * n_left * rows, width)
    left = jnp.dot(left, to_place, preferred_element_type=jnp.bfloat16)
    left = jnp.swapaxes(left.reshape(2 * n_left, rows, width), 0, 1)
    present = jnp.dot(vacancy.astype(jnp.bfloat16), to_place, preferred_element_type=F32)
    present = present.reshape(rows, TILES, LANES)
    recv, left, present = lax.optimization_barrier((recv, left, present))

    edge = HALO * width // piece
    low_mask = present[:HALO].reshape(-1, SUB, LANES)
    high_mask = present[rows - HALO :].reshape(-1, SUB, LANES)
    low = jnp.concatenate([recv[:edge], low_mask])
    high = jnp.concatenate([recv[recv.shape[0] - edge :], high_mask])
    core = lax.axis_index("sites") % 2
    lower_slab = core == 0
    to_chip = [(i, (i + 1 if i % 2 else i - 1) % count) for i in range(count)]
    to_core = [(i, i ^ 1) for i in range(count)]
    across = lax.ppermute(jnp.where(lower_slab, low, high), "sites", to_chip)
    sibling = lax.ppermute(jnp.where(lower_slab, high, low), "sites", to_core)
    core = core.astype(jnp.int32).reshape(1)
    total, edges = inner_moments(recv, present, left)
    total = edge_moments(False, core, sibling, present, left, total, edges)
    total = edge_moments(True, core, across, present, left, total, edges)
    def moved(values, flip):
        return lax.ppermute(values, "sites", [(i, i ^ flip) for i in range(count)])

    total = total + moved(total, 1)
    y_near, z_near, both = moved(total, 8), moved(total, 2), moved(total, 10)
    total = (total + y_near) + (z_near + both)
    y_far, z_far, both = moved(total, 24), moved(total, 4), moved(total, 28)
    out = last_sum(total, y_far, z_far, both).reshape(2, MOM, width_group, n_left)
    return jnp.swapaxes(out, 2, 3)[..., None]


def solution(mesh):
    return jax.shard_map(
        per_device,
        mesh=mesh,
        in_specs=(
            P(None, None, None, None, ("cols", "sites"), None),
            P(None, None, "sites", None),
            P("sites", None),
        ),
        out_specs=P(None, None, None, None, "cols"),
        check_vma=False,
    )
```

```python
import functools

import jax
import jax.numpy as jnp
from jax import lax
from jax.experimental import pallas as pl
from jax.experimental.pallas import tpu as pltpu
from jax.sharding import PartitionSpec as P

MOM = 4
HALO = 4
ONSITE_MASS = 0.3
SECOND_HOP = 0.2
BAND_SCALE = 4.5
LANES = 128
SUB = 8
TILES = 4
F32 = jnp.float32


PACK_GROUPS = 4
MERGES = 16


def pack_kernel(in_ref, out_ref, turned):
    columns, groups, slabs, width = in_ref.shape
    lane = lax.broadcasted_iota(jnp.int32, (SUB, LANES), 1)
    odd, high = lane // width % 2 == 1, lane // width >= 2
    swapped = jnp.where(odd, lane - width, lane + width)
    for k in range(groups):
        for base in range(0, slabs, SUB):
            octets = [
                jnp.swapaxes(in_ref[c : c + SUB, k, base : base + SUB, :], 0, 1)
                for c in range(0, columns, SUB)
            ]
            for half in (0, 4):
                rows = [octet[half + s] for s in range(4) for octet in octets]
                turned[(k * slabs + base + half) // 4] = jnp.concatenate(rows, axis=0).T

    @pl.loop(0, groups * slabs // 4 // MERGES)
    def _(i):
        for j in range(MERGES):
            slot = i * MERGES + j
            v = [turned[slot, pl.ds(t, SUB, stride=TILES), :] for t in range(TILES)]
            for p in (0, 2):
                low, upper = v[p], v[p + 1]
                moved = jnp.take_along_axis(jnp.where(odd, low, upper), swapped, axis=1)
                v[p], v[p + 1] = jnp.where(odd, moved, low), jnp.where(odd, upper, moved)
            for p in (0, 1):
                low, upper = v[p], v[p + 2]
                moved = pltpu.roll(jnp.where(high, low, upper), LANES // 2, 1)
                v[p], v[p + 2] = jnp.where(high, moved, low), jnp.where(high, upper, moved)
            for s in range(4):
                out_ref[slot * 4 // slabs, slot * 4 % slabs + s] = v[s]


def pack(pieces):
    columns, groups, slabs, width = pieces.shape
    step = PACK_GROUPS
    out = pl.pallas_call(
        pack_kernel,
        grid=(groups // step,),
        in_specs=[pl.BlockSpec((columns, step, slabs, width), lambda k: (0, k, 0, 0))],
        out_specs=pl.BlockSpec((step, slabs, SUB, LANES), lambda k: (k, 0, 0, 0)),
        out_shape=jax.ShapeDtypeStruct((groups, slabs, SUB, LANES), F32),
        scratch_shapes=[pltpu.VMEM((step * slabs // 4, width, LANES), F32)],
        name="pack",
    )(pieces)
    return out.reshape(groups * slabs, SUB, LANES)


def wrap_masks():
    lane = lax.broadcasted_iota(jnp.int32, (SUB, LANES), 1)
    return lane == 0, lane == LANES - 1


def ahead(tiles, is_last):
    wrapped = jnp.where(is_last, 0.0, pltpu.roll(tiles[0], LANES - 1, 1))
    return tiles[1:] + [wrapped]


def behind(tiles, is_first):
    wrapped = jnp.where(is_first, 0.0, pltpu.roll(tiles[-1], 1, 1))
    return [wrapped] + tiles[:-1]


def stencil_row(level, parity, below, centre, above, old, mask, wraps):
    is_first, is_last = wraps
    T = range(TILES)
    nxt, prv, second = [], [], []
    for r in (0, 1):
        w = centre[r]
        diag = [above[r][t] + below[r][t] for t in T]
        fore, back = ahead(w, is_last), behind(w, is_first)
        if level == 0:
            a = ahead([2.0 * fore[t] - diag[t] for t in T], is_last)
            b = behind([2.0 * back[t] - diag[t] for t in T], is_first)
            second.append([a[t] + b[t] for t in T])
        else:
            a = ahead([fore[t] - diag[t] for t in T], is_last)
            b = behind([back[t] - diag[t] for t in T], is_first)
            second.append([a[t] - b[t] for t in T])
        nxt.append(fore)
        prv.append(back)
    result = []
    for r in (0, 1):
        values = []
        for t in T:
            sign = 1.0 if (parity + t) % 2 == 0 else -1.0
            if level == 0:
                along = prv[1][t] - nxt[1][t] if r == 0 else nxt[0][t] - prv[0][t]
                total = along - (SECOND_HOP * sign) * second[r][t]
            else:
                vertical = above[r][t] if sign > 0 else below[r][t]
                near = (nxt[r][t] + prv[r][t]) + vertical
                turn = -sign if r == 0 else sign
                total = near + (
                    (ONSITE_MASS * sign) * centre[r][t] + (SECOND_HOP * turn) * second[1 - r][t]
                )
            total = total * mask[t]
            values.append(total - old[r][t] if level > 1 else total)
        result.append(values)
    return result


SCALES = (1.0, 1.0 / BAND_SCALE, 2.0 / BAND_SCALE, 2.0 / BAND_SCALE)


def scaled(level, mask):
    return mask if level == 0 else [SCALES[level] * m for m in mask]


def turn_row(src, first):
    return src[pl.ds(first, 16)].reshape(LANES, LANES).T


def product(acc, blocks, left_ref, y):
    for t in range(TILES):
        zero = jnp.zeros((SUB, LANES), F32)
        stacked = [blocks(r, m, h, t) for r in (0, 1) for m in range(MOM) for h in (0, 1)]
        rhs = jnp.concatenate([zero if b is None else b for b in stacked], axis=0)
        term = lax.dot_general(
            rhs.astype(jnp.bfloat16),
            left_ref[y, :, t * LANES : (t + 1) * LANES],
            (((1,), (1,)), ((), ())),
            preferred_element_type=F32,
        )
        acc = term if acc is None else acc + term
    return acc


def inner_kernel(recv_ref, pres_ref, left_ref, sum_ref, edge_ref, field, presb):
    rows = left_ref.shape[0]
    wraps = wrap_masks()
    T = range(TILES)

    @pl.loop(0, rows // 4)
    def _(i):
        for k in range(4):
            y = 4 * i + k
            turned = turn_row(recv_ref, y * 16)
            for t in T:
                mask = jnp.broadcast_to(pres_ref[y, pl.ds(t, 1), :], (SUB, LANES))
                presb[y, t] = mask
                for q in range(4):
                    at = (4 * t + q) * SUB
                    field[0, y, q // 2, q % 2, t] = turned[at : at + SUB] * mask

    def load(level, y, half):
        return [[field[level, y, r, half, t] for t in T] for r in (0, 1)]

    for level in range(MOM):
        first = level + 1

        @pl.loop(0, (rows - 2 * first) // 2)
        def _(i, level=level, first=first):
            y = first + 2 * i
            masks = [scaled(level, [presb[y + k, t] for t in T]) for k in (0, 1)]
            for half in (0, 1):
                window = [load(level, y + k, half) for k in (-1, 0, 1, 2)]
                for k in (0, 1):
                    old = load(level - 1, y + k, half) if level > 1 else None
                    values = stencil_row(
                        level, (first + k) % 2, *window[k : k + 3], old, masks[k], wraps
                    )
                    for r in (0, 1):
                        for t in T:
                            field[(level + 1) % MOM, y + k, r, half, t] = values[r][t]

    for level in range(MOM):
        edge_ref[level, 0] = field[level, level : level + 2]
        edge_ref[level, 1] = field[level, rows - 2 - level : rows - level]
    acc = None
    for y in range(1, rows - 1):

        def blocks(r, m, half, t, y=y):
            return field[(m + 1) % MOM, y, r, half, t] if m < y < rows - 1 - m else None

        acc = product(acc, blocks, left_ref, y)
    sum_ref[...] = acc


def edge_kernel(across, core_ref, src_ref, pres_ref, left_ref, sum_ref, edge_ref, out_ref, field, presb):
    rows = left_ref.shape[0]
    wraps = wrap_masks()
    T = range(TILES)
    tail = HALO * 16

    def side_sum(side):
        base = (-HALO, rows - 2 * HALO)[side]
        for i in range(HALO):
            j = i if side == 0 else 2 * HALO + i
            turned = turn_row(src_ref, i * 16)
            for t in T:
                at = i * TILES + t
                row = src_ref[tail + at // SUB, pl.ds(at % SUB, 1), :]
                mask = jnp.broadcast_to(row, (SUB, LANES))
                presb[j, t] = mask
                for q in range(4):
                    at = (4 * t + q) * SUB
                    field[0, j, q // 2, q % 2, t] = turned[at : at + SUB] * mask
        for j in range(HALO, 2 * HALO):
            for t in T:
                presb[j, t] = jnp.broadcast_to(pres_ref[base + j, pl.ds(t, 1), :], (SUB, LANES))

        def tile(level, j, r, half, t):
            first = HALO + level if side == 0 else 2 * HALO - 2 - level
            if first <= j < first + 2:
                return edge_ref[level, side, j - first, r, half, t]
            return field[level, j, r, half, t]

        def load(level, j, half):
            return [[tile(level, j, r, half, t) for t in T] for r in (0, 1)]

        for level in range(MOM):
            first = 1 + level if side == 0 else 2 * HALO - 1 - level
            for half in (0, 1):
                window = [load(level, first + k, half) for k in range(-1, 5)]
                for k in range(4):
                    j = first + k
                    mask = scaled(level, [presb[j, t] for t in T])
                    old = load(level - 1, j, half) if level > 1 else None
                    values = stencil_row(level, j % 2, *window[k : k + 3], old, mask, wraps)
                    for r in (0, 1):
                        for t in T:
                            field[(level + 1) % MOM, j, r, half, t] = values[r][t]

        acc = sum_ref[...]
        for y in range(HALO) if side == 0 else range(rows - HALO, rows):

            def blocks(r, m, half, t, y=y):
                if m < y < rows - 1 - m:
                    return None
                return field[(m + 1) % MOM, y - base, r, half, t]

            acc = product(acc, blocks, left_ref, y)
        if across:
            half_rows = MOM * 2 * SUB
            top, bottom = acc[:half_rows], acc[half_rows:]
            lane_out = lax.broadcasted_iota(jnp.int32, top.shape, 1)
            acc = pltpu.roll(bottom, LANES // 2, 1) + jnp.where(lane_out < LANES // 2, top, -top)
        out_ref[...] = acc

    for core in (0, 1):

        @pl.when(core_ref[0] == core)
        def _(side=core if across else 1 - core):
            side_sum(side)


ROW = (2, 2, TILES, SUB, LANES)


def inner_moments(recv, pres, left):
    rows, n2, _ = left.shape
    vm = pl.BlockSpec(memory_space=pltpu.VMEM)
    return pl.pallas_call(
        inner_kernel,
        in_specs=[vm] * 3,
        out_specs=[vm] * 2,
        out_shape=[
            jax.ShapeDtypeStruct((2 * MOM * 2 * SUB, n2), F32),
            jax.ShapeDtypeStruct((MOM, 2, 2, *ROW), F32),
        ],
        scratch_shapes=[
            pltpu.VMEM((MOM, rows, *ROW), F32),
            pltpu.VMEM((rows, TILES, SUB, LANES), F32),
        ],
        compiler_params=pltpu.CompilerParams(vmem_limit_bytes=40 * 2**20),
        cost_estimate=pl.CostEstimate(flops=10**9, bytes_accessed=10**7, transcendentals=0),
        name="inner_moments",
    )(recv, pres, left)


def edge_moments(across, core, src, pres, left, total, edges):
    n2 = left.shape[1]
    vm = pl.BlockSpec(memory_space=pltpu.VMEM)
    return pl.pallas_call(
        functools.partial(edge_kernel, across),
        in_specs=[pl.BlockSpec(memory_space=pltpu.SMEM)] + [vm] * 5,
        out_specs=vm,
        out_shape=jax.ShapeDtypeStruct(((1 if across else 2) * MOM * 2 * SUB, n2), F32),
        scratch_shapes=[
            pltpu.VMEM((MOM, 3 * HALO, *ROW), F32),
            pltpu.VMEM((3 * HALO, TILES, SUB, LANES), F32),
        ],
        compiler_params=pltpu.CompilerParams(vmem_limit_bytes=40 * 2**20),
        cost_estimate=pl.CostEstimate(flops=10**8, bytes_accessed=10**6, transcendentals=0),
        name="edge_across" if across else "edge_sibling",
    )(core, src, pres, left, total, edges)


def last_sum_kernel(mine_ref, far_ref, one_ref, other_ref, out_ref):
    total = (mine_ref[...] + far_ref[...]) + (one_ref[...] + other_ref[...])
    half = out_ref.shape[2]
    out_ref[0] = total[:, :half]
    out_ref[1] = total[:, half:]


def last_sum(mine, far, one, other):
    rows, width = mine.shape
    vm = pl.BlockSpec(memory_space=pltpu.VMEM)
    return pl.pallas_call(
        last_sum_kernel,
        in_specs=[vm] * 4,
        out_specs=vm,
        out_shape=jax.ShapeDtypeStruct((2, rows, width // 2), F32),
        compiler_params=pltpu.CompilerParams(vmem_limit_bytes=8 * 2**20),
        name="last_sum",
    )(mine, far, one, other)


def per_device(right_vectors, left_vectors, vacancy):
    parts, width_group, groups, slabs, _, piece = right_vectors.shape
    count = lax.axis_size("sites")
    n_left, rows, width = left_vectors.shape[1:]

    packed = pack(right_vectors.reshape(parts * width_group, groups, slabs, piece))
    packed, left_vectors = lax.optimization_barrier((packed, left_vectors))
    recv = lax.all_to_all(packed, ("cols", "sites"), 0, 0, tiled=True)

    site = lax.broadcasted_iota(jnp.int32, (width, width), 0)
    place = lax.broadcasted_iota(jnp.int32, (width, width), 1)
    to_place = (site % TILES * LANES + site // TILES == place).astype(jnp.bfloat16)
    left = left_vectors.reshape(2 * n_left * rows, width)
    left = jnp.dot(left, to_place, preferred_element_type=jnp.bfloat16)
    left = jnp.swapaxes(left.reshape(2 * n_left, rows, width), 0, 1)
    present = jnp.dot(vacancy.astype(jnp.bfloat16), to_place, preferred_element_type=F32)
    present = present.reshape(rows, TILES, LANES)
    recv, left, present = lax.optimization_barrier((recv, left, present))

    edge = HALO * width // piece
    low_mask = present[:HALO].reshape(-1, SUB, LANES)
    high_mask = present[rows - HALO :].reshape(-1, SUB, LANES)
    core = lax.axis_index("sites") % 2
    to_chip = [(i, (i + 1 if i % 2 else i - 1) % count) for i in range(count)]
    to_core = [(i, i ^ 1) for i in range(count)]
    masks = jnp.concatenate([low_mask, high_mask])

    def edge_rows(side):
        tiles = lax.dynamic_slice_in_dim(recv, side * (recv.shape[0] - edge), edge)
        mask = lax.dynamic_slice_in_dim(masks, side * low_mask.shape[0], low_mask.shape[0])
        return jnp.concatenate([tiles, mask])

    across = lax.ppermute(edge_rows(core), "sites", to_chip)
    sibling = lax.ppermute(edge_rows(1 - core), "sites", to_core)
    core = core.astype(jnp.int32).reshape(1)
    total, edges = inner_moments(recv, present, left)
    total = edge_moments(False, core, sibling, present, left, total, edges)
    total = edge_moments(True, core, across, present, left, total, edges)
    def moved(values, flip):
        return lax.ppermute(values, "sites", [(i, i ^ flip) for i in range(count)])

    total = total + moved(total, 1)
    z_near, y_near, both = moved(total, 2), moved(total, 8), moved(total, 10)
    total = (total + z_near) + (y_near + both)
    z_far, y_far, both = moved(total, 4), moved(total, 24), moved(total, 28)
    out = last_sum(total, z_far, y_far, both).reshape(2, MOM, width_group, n_left)
    return jnp.swapaxes(out, 2, 3)[..., None]


def solution(mesh):
    return jax.shard_map(
        per_device,
        mesh=mesh,
        in_specs=(
            P(None, None, None, None, ("cols", "sites"), None),
            P(None, None, "sites", None),
            P("sites", None),
        ),
        out_specs=P(None, None, None, None, "cols"),
        check_vma=False,
    )
```

```python
import functools

import jax
import jax.numpy as jnp
from jax import lax
from jax.experimental import pallas as pl
from jax.experimental.pallas import tpu as pltpu
from jax.sharding import PartitionSpec as P

MOM = 4
HALO = 4
ONSITE_MASS = 0.3
SECOND_HOP = 0.2
BAND_SCALE = 4.5
LANES = 128
SUB = 8
TILES = 4
F32 = jnp.float32


PACK_GROUPS = 4
MERGES = 16


def pack_kernel(in_ref, out_ref, turned):
    columns, groups, slabs, width = in_ref.shape
    lane = lax.broadcasted_iota(jnp.int32, (SUB, LANES), 1)
    odd, high = lane // width % 2 == 1, lane // width >= 2
    swapped = jnp.where(odd, lane - width, lane + width)
    for k in range(groups):
        for base in range(0, slabs, SUB):
            octets = [
                jnp.swapaxes(in_ref[c : c + SUB, k, base : base + SUB, :], 0, 1)
                for c in range(0, columns, SUB)
            ]
            for half in (0, 4):
                rows = [octet[half + s] for s in range(4) for octet in octets]
                turned[(k * slabs + base + half) // 4] = jnp.concatenate(rows, axis=0).T

    @pl.loop(0, groups * slabs // 4 // MERGES)
    def _(i):
        every = [
            [turned[i * MERGES + j, pl.ds(t, SUB, stride=TILES), :] for t in range(TILES)]
            for j in range(MERGES)
        ]
        for v in every:
            for p in (0, 2):
                low, upper = v[p], v[p + 1]
                moved = jnp.take_along_axis(jnp.where(odd, low, upper), swapped, axis=1)
                v[p], v[p + 1] = jnp.where(odd, moved, low), jnp.where(odd, upper, moved)
        for v in every:
            for p in (0, 1):
                low, upper = v[p], v[p + 2]
                moved = pltpu.roll(jnp.where(high, low, upper), LANES // 2, 1)
                v[p], v[p + 2] = jnp.where(high, moved, low), jnp.where(high, upper, moved)
        for j, v in enumerate(every):
            slot = i * MERGES + j
            for s in range(4):
                out_ref[slot * 4 // slabs, slot * 4 % slabs + s] = v[s]


def pack(pieces):
    columns, groups, slabs, width = pieces.shape
    step = PACK_GROUPS
    out = pl.pallas_call(
        pack_kernel,
        grid=(groups // step,),
        in_specs=[pl.BlockSpec((columns, step, slabs, width), lambda k: (0, k, 0, 0))],
        out_specs=pl.BlockSpec((step, slabs, SUB, LANES), lambda k: (k, 0, 0, 0)),
        out_shape=jax.ShapeDtypeStruct((groups, slabs, SUB, LANES), F32),
        scratch_shapes=[pltpu.VMEM((step * slabs // 4, width, LANES), F32)],
        name="pack",
    )(pieces)
    return out.reshape(groups * slabs, SUB, LANES)


def wrap_masks():
    lane = lax.broadcasted_iota(jnp.int32, (SUB, LANES), 1)
    return lane == 0, lane == LANES - 1


def ahead(tiles, is_last):
    wrapped = jnp.where(is_last, 0.0, pltpu.roll(tiles[0], LANES - 1, 1))
    return tiles[1:] + [wrapped]


def behind(tiles, is_first):
    wrapped = jnp.where(is_first, 0.0, pltpu.roll(tiles[-1], 1, 1))
    return [wrapped] + tiles[:-1]


def stencil_row(level, parity, below, centre, above, old, mask, wraps):
    is_first, is_last = wraps
    T = range(TILES)
    nxt, prv, second = [], [], []
    for r in (0, 1):
        w = centre[r]
        diag = [above[r][t] + below[r][t] for t in T]
        fore, back = ahead(w, is_last), behind(w, is_first)
        if level == 0:
            a = ahead([2.0 * fore[t] - diag[t] for t in T], is_last)
            b = behind([2.0 * back[t] - diag[t] for t in T], is_first)
            second.append([a[t] + b[t] for t in T])
        else:
            a = ahead([fore[t] - diag[t] for t in T], is_last)
            b = behind([back[t] - diag[t] for t in T], is_first)
            second.append([a[t] - b[t] for t in T])
        nxt.append(fore)
        prv.append(back)
    result = []
    for r in (0, 1):
        values = []
        for t in T:
            sign = 1.0 if (parity + t) % 2 == 0 else -1.0
            if level == 0:
                along = prv[1][t] - nxt[1][t] if r == 0 else nxt[0][t] - prv[0][t]
                total = along - (SECOND_HOP * sign) * second[r][t]
            else:
                vertical = above[r][t] if sign > 0 else below[r][t]
                near = (nxt[r][t] + prv[r][t]) + vertical
                turn = -sign if r == 0 else sign
                total = near + (
                    (ONSITE_MASS * sign) * centre[r][t] + (SECOND_HOP * turn) * second[1 - r][t]
                )
            total = total * mask[t]
            values.append(total - old[r][t] if level > 1 else total)
        result.append(values)
    return result


SCALES = (1.0, 1.0 / BAND_SCALE, 2.0 / BAND_SCALE, 2.0 / BAND_SCALE)


def scaled(level, mask):
    return mask if level == 0 else [SCALES[level] * m for m in mask]


def turn_row(src, first):
    return src[pl.ds(first, 16)].reshape(LANES, LANES).T


def product(acc, blocks, left_ref, y):
    for t in range(TILES):
        zero = jnp.zeros((SUB, LANES), F32)
        stacked = [blocks(r, m, h, t) for r in (0, 1) for m in range(MOM) for h in (0, 1)]
        rhs = jnp.concatenate([zero if b is None else b for b in stacked], axis=0)
        term = lax.dot_general(
            rhs.astype(jnp.bfloat16),
            left_ref[y, :, t * LANES : (t + 1) * LANES],
            (((1,), (1,)), ((), ())),
            preferred_element_type=F32,
        )
        acc = term if acc is None else acc + term
    return acc


def inner_kernel(recv_ref, pres_ref, left_ref, sum_ref, edge_ref, field, presb):
    rows = left_ref.shape[0]
    wraps = wrap_masks()
    T = range(TILES)

    @pl.loop(0, rows // 4)
    def _(i):
        for k in range(4):
            y = 4 * i + k
            turned = turn_row(recv_ref, y * 16)
            for t in T:
                mask = jnp.broadcast_to(pres_ref[y, pl.ds(t, 1), :], (SUB, LANES))
                presb[y, t] = mask
                for q in range(4):
                    at = (4 * t + q) * SUB
                    field[0, y, q // 2, q % 2, t] = turned[at : at + SUB] * mask

    def load(level, y, half):
        return [[field[level, y, r, half, t] for t in T] for r in (0, 1)]

    for level in range(MOM):
        first = level + 1

        @pl.loop(0, (rows - 2 * first) // 2)
        def _(i, level=level, first=first):
            y = first + 2 * i
            masks = [scaled(level, [presb[y + k, t] for t in T]) for k in (0, 1)]
            for half in (0, 1):
                window = [load(level, y + k, half) for k in (-1, 0, 1, 2)]
                for k in (0, 1):
                    old = load(level - 1, y + k, half) if level > 1 else None
                    values = stencil_row(
                        level, (first + k) % 2, *window[k : k + 3], old, masks[k], wraps
                    )
                    for r in (0, 1):
                        for t in T:
                            field[(level + 1) % MOM, y + k, r, half, t] = values[r][t]

    for level in range(MOM):
        edge_ref[level, 0] = field[level, level : level + 2]
        edge_ref[level, 1] = field[level, rows - 2 - level : rows - level]
    acc = None
    for y in range(1, rows - 1):

        def blocks(r, m, half, t, y=y):
            return field[(m + 1) % MOM, y, r, half, t] if m < y < rows - 1 - m else None

        acc = product(acc, blocks, left_ref, y)
    sum_ref[...] = acc


def edge_kernel(across, core_ref, src_ref, pres_ref, left_ref, sum_ref, edge_ref, out_ref, field, presb):
    rows = left_ref.shape[0]
    wraps = wrap_masks()
    T = range(TILES)
    tail = HALO * 16

    def side_sum(side):
        base = (-HALO, rows - 2 * HALO)[side]
        for i in range(HALO):
            j = i if side == 0 else 2 * HALO + i
            turned = turn_row(src_ref, i * 16)
            for t in T:
                at = i * TILES + t
                row = src_ref[tail + at // SUB, pl.ds(at % SUB, 1), :]
                mask = jnp.broadcast_to(row, (SUB, LANES))
                presb[j, t] = mask
                for q in range(4):
                    at = (4 * t + q) * SUB
                    field[0, j, q // 2, q % 2, t] = turned[at : at + SUB] * mask
        for j in range(HALO, 2 * HALO):
            for t in T:
                presb[j, t] = jnp.broadcast_to(pres_ref[base + j, pl.ds(t, 1), :], (SUB, LANES))

        def tile(level, j, r, half, t):
            first = HALO + level if side == 0 else 2 * HALO - 2 - level
            if first <= j < first + 2:
                return edge_ref[level, side, j - first, r, half, t]
            return field[level, j, r, half, t]

        def load(level, j, half):
            return [[tile(level, j, r, half, t) for t in T] for r in (0, 1)]

        for level in range(MOM):
            first = 1 + level if side == 0 else 2 * HALO - 1 - level
            for half in (0, 1):
                window = [load(level, first + k, half) for k in range(-1, 5)]
                for k in range(4):
                    j = first + k
                    mask = scaled(level, [presb[j, t] for t in T])
                    old = load(level - 1, j, half) if level > 1 else None
                    values = stencil_row(level, j % 2, *window[k : k + 3], old, mask, wraps)
                    for r in (0, 1):
                        for t in T:
                            field[(level + 1) % MOM, j, r, half, t] = values[r][t]

        acc = sum_ref[...]
        for y in range(HALO) if side == 0 else range(rows - HALO, rows):

            def blocks(r, m, half, t, y=y):
                if m < y < rows - 1 - m:
                    return None
                return field[(m + 1) % MOM, y - base, r, half, t]

            acc = product(acc, blocks, left_ref, y)
        if across:
            half_rows = MOM * 2 * SUB
            top, bottom = acc[:half_rows], acc[half_rows:]
            lane_out = lax.broadcasted_iota(jnp.int32, top.shape, 1)
            acc = pltpu.roll(bottom, LANES // 2, 1) + jnp.where(lane_out < LANES // 2, top, -top)
        out_ref[...] = acc

    for core in (0, 1):

        @pl.when(core_ref[0] == core)
        def _(side=core if across else 1 - core):
            side_sum(side)


ROW = (2, 2, TILES, SUB, LANES)


def inner_moments(recv, pres, left):
    rows, n2, _ = left.shape
    vm = pl.BlockSpec(memory_space=pltpu.VMEM)
    return pl.pallas_call(
        inner_kernel,
        in_specs=[vm] * 3,
        out_specs=[vm] * 2,
        out_shape=[
            jax.ShapeDtypeStruct((2 * MOM * 2 * SUB, n2), F32),
            jax.ShapeDtypeStruct((MOM, 2, 2, *ROW), F32),
        ],
        scratch_shapes=[
            pltpu.VMEM((MOM, rows, *ROW), F32),
            pltpu.VMEM((rows, TILES, SUB, LANES), F32),
        ],
        compiler_params=pltpu.CompilerParams(vmem_limit_bytes=40 * 2**20),
        cost_estimate=pl.CostEstimate(flops=10**9, bytes_accessed=10**7, transcendentals=0),
        name="inner_moments",
    )(recv, pres, left)


def edge_moments(across, core, src, pres, left, total, edges):
    n2 = left.shape[1]
    vm = pl.BlockSpec(memory_space=pltpu.VMEM)
    return pl.pallas_call(
        functools.partial(edge_kernel, across),
        in_specs=[pl.BlockSpec(memory_space=pltpu.SMEM)] + [vm] * 5,
        out_specs=vm,
        out_shape=jax.ShapeDtypeStruct(((1 if across else 2) * MOM * 2 * SUB, n2), F32),
        scratch_shapes=[
            pltpu.VMEM((MOM, 3 * HALO, *ROW), F32),
            pltpu.VMEM((3 * HALO, TILES, SUB, LANES), F32),
        ],
        compiler_params=pltpu.CompilerParams(vmem_limit_bytes=40 * 2**20),
        cost_estimate=pl.CostEstimate(flops=10**8, bytes_accessed=10**6, transcendentals=0),
        name="edge_across" if across else "edge_sibling",
    )(core, src, pres, left, total, edges)


def last_sum_kernel(mine_ref, far_ref, one_ref, other_ref, out_ref):
    total = (mine_ref[...] + far_ref[...]) + (one_ref[...] + other_ref[...])
    half = out_ref.shape[2]
    out_ref[0] = total[:, :half]
    out_ref[1] = total[:, half:]


def last_sum(mine, far, one, other):
    rows, width = mine.shape
    vm = pl.BlockSpec(memory_space=pltpu.VMEM)
    return pl.pallas_call(
        last_sum_kernel,
        in_specs=[vm] * 4,
        out_specs=vm,
        out_shape=jax.ShapeDtypeStruct((2, rows, width // 2), F32),
        compiler_params=pltpu.CompilerParams(vmem_limit_bytes=8 * 2**20),
        name="last_sum",
    )(mine, far, one, other)


def per_device(right_vectors, left_vectors, vacancy):
    parts, width_group, groups, slabs, _, piece = right_vectors.shape
    count = lax.axis_size("sites")
    n_left, rows, width = left_vectors.shape[1:]

    packed = pack(right_vectors.reshape(parts * width_group, groups, slabs, piece))
    packed, left_vectors = lax.optimization_barrier((packed, left_vectors))
    recv = lax.all_to_all(packed, ("cols", "sites"), 0, 0, tiled=True)

    site = lax.broadcasted_iota(jnp.int32, (width, width), 0)
    place = lax.broadcasted_iota(jnp.int32, (width, width), 1)
    to_place = (site % TILES * LANES + site // TILES == place).astype(jnp.bfloat16)
    left = left_vectors.reshape(2 * n_left * rows, width)
    left = jnp.dot(left, to_place, preferred_element_type=jnp.bfloat16)
    left = jnp.swapaxes(left.reshape(2 * n_left, rows, width), 0, 1)
    present = jnp.dot(vacancy.astype(jnp.bfloat16), to_place, preferred_element_type=F32)
    present = present.reshape(rows, TILES, LANES)
    recv, left, present = lax.optimization_barrier((recv, left, present))

    edge = HALO * width // piece
    low_mask = present[:HALO].reshape(-1, SUB, LANES)
    high_mask = present[rows - HALO :].reshape(-1, SUB, LANES)
    low = jnp.concatenate([recv[:edge], low_mask])
    high = jnp.concatenate([recv[recv.shape[0] - edge :], high_mask])
    core = lax.axis_index("sites") % 2
    lower_slab = core == 0
    to_chip = [(i, (i + 1 if i % 2 else i - 1) % count) for i in range(count)]
    to_core = [(i, i ^ 1) for i in range(count)]
    across = lax.ppermute(jnp.where(lower_slab, low, high), "sites", to_chip)
    sibling = lax.ppermute(jnp.where(lower_slab, high, low), "sites", to_core)
    core = core.astype(jnp.int32).reshape(1)
    total, edges = inner_moments(recv, present, left)
    total = edge_moments(False, core, sibling, present, left, total, edges)
    total = edge_moments(True, core, across, present, left, total, edges)
    def moved(values, flip):
        return lax.ppermute(values, "sites", [(i, i ^ flip) for i in range(count)])

    total = total + moved(total, 1)
    z_near, y_near, both = moved(total, 2), moved(total, 8), moved(total, 10)
    total = (total + z_near) + (y_near + both)
    z_far, y_far, both = moved(total, 4), moved(total, 24), moved(total, 28)
    out = last_sum(total, z_far, y_far, both).reshape(2, MOM, width_group, n_left)
    return jnp.swapaxes(out, 2, 3)[..., None]


def solution(mesh):
    return jax.shard_map(
        per_device,
        mesh=mesh,
        in_specs=(
            P(None, None, None, None, ("cols", "sites"), None),
            P(None, None, "sites", None),
            P("sites", None),
        ),
        out_specs=P(None, None, None, None, "cols"),
        check_vma=False,
    )
```
